1024 devices in a mesh: gx: 32 (over z, x_lo), gy: 4 (over x_hi, core), gz: 8 (over y).
Axes of the slice: x: 8 (x_hi: 2, x_lo: 4; x = x_hi * 4 + x_lo), y: 8, z: 8, core: 2. Of those that a mesh axis runs over, the one named last changes fastest.
Arguments:
- coefficients: bfloat16 [8, 256, 32, 64, 256], P(None, 'gx', 'gy', 'gz'), may hold values from -6 to 6
- fun_count: int32 [32, 4, 8], P('gx', 'gy', 'gz'), may hold values from 64 to 256, as said below
- tile_offset: int32 [32, 4, 8], P('gx', 'gy', 'gz'), may hold values from -1 to 1
- kernel: bfloat16 [32, 256, 256], P('gx'), may hold values from -0.0234375 to 0.0234375
Outputs:
- density: float32 [32, 4, 8, 4096], P('gx', 'gy', 'gz')
The draws below stay inside these ranges and needn't reach their ends.
Inputs may be any that keep to these rules, and one draw needn't show every extreme that they name: `fun_count`: the slots below a domain's count hold its support functions; the other slots are empty. Some domain has all 256 slots live. `tile_offset`: the kernel tile of a domain is held by the first domain index that differs from its own by the offset, cyclically.
All inputs are finite; a program needn't handle non-finite values.
Results may differ from the reference program's by a relative error of at most 0.007.
Values may be sent and summed in bfloat16 or wider, within the bound.
No kernel may reach another device: no remote copies, remote signals or barrier semaphores. Data moves between devices by JAX's collectives and lax.ppermute only.
A program may use at most 32 MiB of HBM per device.

```python
import jax
import jax.numpy as jnp
from jax import lax

CX = 8
CY = 8
CZ = 8
F = 256
DOM_X = 32
DOM_Y = 4
DOM_Z = 8
NX = 256
NY = 32
NZ = 64
CELLS = 4096


def draw_fun_count(key, part):
    counts = jax.random.randint(jax.random.fold_in(key, 11), (DOM_X * DOM_Y * DOM_Z,), F // 4, F + 1)
    chosen = jax.random.randint(jax.random.fold_in(key, 12), (), 0, DOM_X * DOM_Y * DOM_Z)
    positions = jnp.arange(DOM_X * DOM_Y * DOM_Z, dtype=jnp.int32)
    counts = jnp.where(positions == chosen, F, counts)
    return counts.reshape(DOM_X, DOM_Y, DOM_Z).astype(jnp.int32)


def plant(drawn, own_key, least, top_value):
    place = [jax.random.randint(jax.random.fold_in(own_key, axis), (), 0, length) for axis, length in enumerate(drawn.shape)]
    main_axis = drawn.shape.index(max(drawn.shape))
    beside = place[:main_axis] + [(place[main_axis] + 1) % drawn.shape[main_axis]] + place[main_axis + 1:]
    return drawn.at[tuple(place)].set(least).at[tuple(beside)].set(top_value)


def level_of(rng, shape, split, smallest, largest):
    gain = 1.0
    for dim, blocks in split:
        steps = jax.random.uniform(jax.random.fold_in(jax.random.fold_in(rng, 6), dim), (blocks,), jnp.float32, smallest / len(split), largest / len(split))
        gain = gain * jnp.repeat(jnp.exp(steps), shape[dim] // blocks).reshape((-1,) + (1,) * (len(shape) - 1 - dim))
    return gain


def bell_draw(stream_key, dims, deviation, most, cuts=(), held_as=jnp.bfloat16):
    gain = level_of(stream_key, dims, cuts, -0.22, 0.18) if cuts else 1.0
    values = jax.random.normal(stream_key, dims, jnp.float32) * deviation * gain
    return jnp.minimum(jnp.maximum(values, -most), most).astype(held_as)


def setup_inputs(seed: int = 0) -> dict:
    keys = jax.random.split(jax.random.key(seed), 5)
    coefficients = bell_draw(keys[0], (8, NX, NY, NZ, F), 1.0, 6.0, ((1, 32), (2, 4), (3, 8)))
    fun_count = draw_fun_count(jax.random.fold_in(keys[4], 71), 0)
    tile_offset = plant(jax.random.randint(keys[2], (DOM_X, DOM_Y, DOM_Z), -1, 2), jax.random.fold_in(keys[2], 1), -1, 1).astype(jnp.int32)
    kernel = bell_draw(keys[3], (DOM_X, F, F), (F * F) ** -0.5, 0.0234375, ((0, 32),))
    return {"coefficients": coefficients, "fun_count": fun_count, "tile_offset": tile_offset, "kernel": kernel}


FILT = [0.48296291314453416, 0.8365163037378079, 0.22414386804201339, -0.12940952255126037]
WAVE = [(1.0 if t % 2 == 0 else -1.0) * FILT[3 - t] for t in range(4)]


def band_table(coarse):
    fine_idx = jnp.arange(2 * coarse, dtype=jnp.int32)[:, None]
    coarse_idx = jnp.arange(coarse + 2, dtype=jnp.int32)[None, :]
    offset = fine_idx - 2 * coarse_idx + 3
    low = jnp.zeros(offset.shape, jnp.float32)
    high = jnp.zeros(offset.shape, jnp.float32)
    for tap in range(4):
        low = low + jnp.where(offset == tap, FILT[tap], 0.0).astype(jnp.float32)
        high = high + jnp.where(offset == tap, WAVE[tap], 0.0).astype(jnp.float32)
    return jnp.stack([low, high])


def synthesize(box, table_x, table_y, table_z):
    high = lax.Precision.HIGHEST
    data = box.astype(jnp.float32)
    data = data.reshape((2, 4) + data.shape[1:])
    after_x = jnp.einsum("cnk,cpkyzf->pnyzf", table_x, data, precision=high).astype(jnp.bfloat16)
    data = after_x.astype(jnp.float32)
    data = data.reshape((2, 2) + data.shape[1:])
    after_y = jnp.einsum("cnk,cpxkzf->pxnzf", table_y, data, precision=high).astype(jnp.bfloat16)
    data = after_y.astype(jnp.float32)
    return jnp.einsum("cnk,cxykf->xynf", table_z, data, precision=high).astype(jnp.bfloat16)


def reference(coefficients, fun_count, tile_offset, kernel):
    live_count = jnp.repeat(jnp.repeat(jnp.repeat(fun_count, CX, axis=0), CY, axis=1), CZ, axis=2)
    slots = jnp.arange(F, dtype=jnp.int32)
    mask = slots[None, None, None, :] < live_count[:, :, :, None]
    live = jnp.where(mask[None], coefficients, jnp.zeros((), jnp.bfloat16))
    padded = jnp.pad(live, ((0, 0), (1, 1), (1, 1), (1, 1), (0, 0)))
    table_x = band_table(CX)
    table_y = band_table(CY)
    table_z = band_table(CZ)

    def one_domain(index):
        dom_x = index // (DOM_Y * DOM_Z)
        dom_y = (index // DOM_Z) % DOM_Y
        dom_z = index % DOM_Z
        zero = jnp.zeros((), jnp.int32)
        box = lax.dynamic_slice(padded, (zero, (dom_x * CX).astype(jnp.int32), (dom_y * CY).astype(jnp.int32), (dom_z * CZ).astype(jnp.int32), zero), (8, CX + 2, CY + 2, CZ + 2, F))
        phi = synthesize(box, table_x, table_y, table_z).reshape(CELLS, F)
        owner = ((dom_x + tile_offset[dom_x, dom_y, dom_z]) % DOM_X).astype(jnp.int32)
        tile = lax.dynamic_index_in_dim(kernel, owner, 0, keepdims=False)
        psi = jnp.dot(phi, tile, preferred_element_type=jnp.float32)
        return jnp.sum(phi.astype(jnp.float32) * psi, axis=1)

    density = lax.map(one_domain, jnp.arange(DOM_X * DOM_Y * DOM_Z, dtype=jnp.int32))
    return density.reshape(DOM_X, DOM_Y, DOM_Z, CELLS)
```

```python
import functools

import jax
import jax.numpy as jnp
import ml_dtypes
import numpy as np
from jax import lax
from jax.experimental import pallas as pl
from jax.experimental.pallas import tpu as pltpu
from jax.sharding import PartitionSpec as P

FILT = [0.48296291314453416, 0.8365163037378079, 0.2241438680420134, -0.12940952255126037]
WAVE = [(1.0 if t % 2 == 0 else -1.0) * FILT[3 - t] for t in range(4)]
AXES = ("gx", "gy", "gz")
F32, BF16 = jnp.float32, jnp.bfloat16


def band_table(coarse):
    table = np.zeros((2, 2 * coarse, coarse))
    for fine in range(2 * coarse):
        for point in range(coarse):
            tap = fine - 2 * point + 1
            if 0 <= tap <= 3:
                table[0, fine, point] = FILT[tap]
                table[1, fine, point] = WAVE[tap]
    return table


def make_tables(cy, cz):
    ty, tz = band_table(cy), band_table(cz)
    fy, fz = 2 * cy, 2 * cz
    inner = np.einsum("cnk,dml->nmcdkl", ty, tz).reshape(fy * fz, 4 * cy * cz)
    ends = {}
    for name, plane, tap in (("first", 0, 0), ("last", cz - 1, 3)):
        pick = np.zeros((2, cz))
        pick[0, plane], pick[1, plane] = FILT[tap], WAVE[tap]
        own = np.einsum("cnk,dl->ncdkl", ty, pick).reshape(fy, 4 * cy * cz)
        before = np.zeros((fy, 2 * cz))
        before[0] = pick.reshape(-1)
        after = np.zeros((fy, 2 * cz))
        after[fy - 1] = pick.reshape(-1)
        ends[name] = (own, before, after)
    halo_y = {}
    for name, row in (("before", 0), ("after", fy - 1)):
        block = np.zeros((fy, fz, 2 * cz))
        block[row] = np.transpose(tz, (1, 0, 2)).reshape(fz, 2 * cz)
        halo_y[name] = block.reshape(fy * fz, 2 * cz)
    halo_z = {}
    for name, column in (("before", 0), ("after", fz - 1)):
        block = np.zeros((fy, fz, fy))
        for row in range(fy):
            block[row, column, row] = 1.0
        halo_z[name] = block.reshape(fy * fz, fy)
    text, mzh, th = [], [], []
    for pz in range(2):
        order = ("last", "first") if pz == 0 else ("first", "last")
        text.append(np.concatenate([inner] + [ends[o][0] for o in order]))
    for py in range(2):
        for pz in range(2):
            order = ("last", "first") if pz == 0 else ("first", "last")
            sides_y = ("after", "before") if py == 0 else ("before", "after")
            sides_z = ("after", "before") if pz == 0 else ("before", "after")
            which = {"before": 1, "after": 2}
            mzh.append(np.concatenate([np.concatenate([ends[o][which[s]] for s in sides_y], axis=1) for o in order]))
            th.append(np.concatenate([halo_y[s] for s in sides_y] + [halo_z[s] for s in sides_z], axis=1))
    cast = lambda parts: np.stack(parts).astype(np.float32).astype(ml_dtypes.bfloat16)
    return cast(text), cast(mzh), cast(th)


def swap_pairs(shape, axis, near):
    out = []
    for place in np.ndindex(*shape):
        other = list(place)
        other[axis] = place[axis] ^ 1 if near else ((place[axis] - 1) ^ 1) + 1
        if 0 <= other[axis] < shape[axis]:
            out.append((int(np.ravel_multi_index(place, shape)), int(np.ravel_multi_index(other, shape))))
    return out


def tile_pairs(shape):
    nx, ny, nz = shape
    index = lambda x, y, z: int(np.ravel_multi_index((x % nx, y, z), shape))
    out = []
    for x, y, z in np.ndindex(*shape):
        step = 1 if y % 2 == 0 else -1
        if x == 0 and ny == 4:
            continue
        out.append((index(x, y, z), index(x + step, y, z)))
    if ny == 4:
        for z in range(nz):
            out.append((index(0, 0, z), index(1, 0, z)))
            out.append((index(0, 1, z), index(1, 2, z)))
        senders = [index(0, y, z) for z in range(nz) for y in (3, 2)]
        takers = [index(nx - 1, y, z) for z in range(nz) for y in (1, 3)]
        out += list(zip(senders, takers))
    return out


def parity(axis):
    return lax.rem(lax.axis_index(axis), 2)


def lane_mask(count_ref, rows, lanes):
    return lax.broadcasted_iota(jnp.int32, (rows, lanes), 1) < count_ref[0]


def faces_kernel(count_ref, c_ref, near_ref, far_ref):
    last_k, rows = c_ref.shape[1] - 1, c_ref.shape[2]
    even = parity("gx") == 0
    mask = lane_mask(count_ref, rows, c_ref.shape[3])
    for b in range(4):
        first = FILT[0] * c_ref[b, 0].astype(F32) + WAVE[0] * c_ref[4 + b, 0].astype(F32)
        last = FILT[3] * c_ref[b, last_k].astype(F32) + WAVE[3] * c_ref[4 + b, last_k].astype(F32)
        first, last = jnp.where(mask, first, 0.0), jnp.where(mask, last, 0.0)
        near_ref[b * rows : (b + 1) * rows] = jnp.where(even, last, first).astype(BF16)
        far_ref[b * rows : (b + 1) * rows] = jnp.where(even, first, last).astype(BF16)


def inner_kernel(count_ref, c_ref, text_ref, x_ref, p_ref, z_ref):
    rows = c_ref.shape[2]
    mask = lane_mask(count_ref, rows, c_ref.shape[3])
    pz = parity("gz")
    cells = p_ref.shape[1]
    for m in range(1, c_ref.shape[1]):
        odd, even = [], []
        for b in range(4):
            s0, w0 = c_ref[b, m - 1].astype(F32), c_ref[4 + b, m - 1].astype(F32)
            s1, w1 = c_ref[b, m].astype(F32), c_ref[4 + b, m].astype(F32)
            o = FILT[2] * s0 + WAVE[2] * w0 + FILT[0] * s1 + WAVE[0] * w1
            e = FILT[3] * s0 + WAVE[3] * w0 + FILT[1] * s1 + WAVE[1] * w1
            odd.append(jnp.where(mask, o, 0.0).astype(BF16))
            even.append(jnp.where(mask, e, 0.0).astype(BF16))
        for i, parts in ((2 * m - 2, odd), (2 * m - 1, even)):
            x = jnp.concatenate(parts, axis=0)
            x_ref[i] = x
            r = jnp.dot(text_ref[pz], x, preferred_element_type=F32)
            p_ref[i] = r[:cells]
            z_ref[i] = r[cells:]


def edge_kernel(count_ref, c_ref, near_ref, far_ref, x_ref, edge_ref, ynear_ref, yfar_ref, *, cy, cz):
    last_k, rows = c_ref.shape[1] - 1, c_ref.shape[2]
    mask = lane_mask(count_ref, rows, c_ref.shape[3])
    even = parity("gx") == 0
    for b in range(4):
        near, far = near_ref[b * rows : (b + 1) * rows].astype(F32), far_ref[b * rows : (b + 1) * rows].astype(F32)
        before, after = jnp.where(even, far, near), jnp.where(even, near, far)
        s0, w0 = c_ref[b, 0].astype(F32), c_ref[4 + b, 0].astype(F32)
        s1, w1 = c_ref[b, last_k].astype(F32), c_ref[4 + b, last_k].astype(F32)
        lo = jnp.where(mask, FILT[1] * s0 + WAVE[1] * w0, 0.0) + before
        hi = jnp.where(mask, FILT[2] * s1 + WAVE[2] * w1, 0.0) + after
        edge_ref[0, b * rows : (b + 1) * rows] = lo.astype(BF16)
        edge_ref[1, b * rows : (b + 1) * rows] = hi.astype(BF16)
    even_y = parity("gy") == 0
    fine = x_ref.shape[0] + 2
    for n in range(fine):
        ref, i = (edge_ref, 0) if n == 0 else (edge_ref, 1) if n == fine - 1 else (x_ref, n - 1)
        near_rows, far_rows = [], []
        for zb in range(2):
            low, high = zb * rows, (2 + zb) * rows
            end = (cy - 1) * cz
            first = FILT[0] * ref[i, low : low + cz].astype(F32) + WAVE[0] * ref[i, high : high + cz].astype(F32)
            last = FILT[3] * ref[i, low + end : low + end + cz].astype(F32) + WAVE[3] * ref[i, high + end : high + end + cz].astype(F32)
            near_rows.append(jnp.where(even_y, last, first))
            far_rows.append(jnp.where(even_y, first, last))
        ynear_ref[n * 2 * cz : (n + 1) * 2 * cz] = jnp.concatenate(near_rows, axis=0).astype(BF16)
        yfar_ref[n * 2 * cz : (n + 1) * 2 * cz] = jnp.concatenate(far_rows, axis=0).astype(BF16)


def edge_cells_kernel(edge_ref, text_ref, p_ref, z_ref):
    pz = parity("gz")
    cells = p_ref.shape[1]
    for i in range(2):
        r = jnp.dot(text_ref[pz], edge_ref[i], preferred_element_type=F32)
        p_ref[i] = r[:cells]
        z_ref[i] = r[cells:]


def zfaces_kernel(ynear_ref, yfar_ref, z_ref, ze_ref, mzh_ref, near_ref, far_ref):
    case = 2 * parity("gy") + parity("gz")
    fine = z_ref.shape[0] + 2
    step = ynear_ref.shape[0] // fine
    half = z_ref.shape[1] // 2
    for n in range(fine):
        own = ze_ref[0] if n == 0 else ze_ref[1] if n == fine - 1 else z_ref[n - 1]
        rows = slice(n * step, (n + 1) * step)
        halo = jnp.concatenate([ynear_ref[rows], yfar_ref[rows]], axis=0)
        r = own + jnp.dot(mzh_ref[case], halo, preferred_element_type=F32)
        near_ref[n * half : (n + 1) * half] = r[:half].astype(BF16)
        far_ref[n * half : (n + 1) * half] = r[half:].astype(BF16)


def density_kernel(offset_ref, own_ref, tile1_ref, tile2_ref, p_ref, pe_ref, th_ref, *rest):
    halos, out_ref, k_ref = rest[:4], rest[4], rest[5]
    case = 2 * parity("gy") + parity("gz")
    even = parity("gy") == 0
    offset = offset_ref[0]
    first, second = tile1_ref[...], tile2_ref[...]
    before, after = jnp.where(even, first, second), jnp.where(even, second, first)
    k_ref[...] = jnp.where(offset == -1, before, jnp.where(offset == 1, after, own_ref[...]))
    fine = p_ref.shape[0] + 2
    lanes = k_ref.shape[1] // 2
    ones = jnp.ones((8, lanes), BF16)
    step = halos[0].shape[0] // fine
    for n in range(fine):
        own = pe_ref[0] if n == 0 else pe_ref[1] if n == fine - 1 else p_ref[n - 1]
        rows = slice(n * step, (n + 1) * step)
        halo = jnp.concatenate([h[rows] for h in halos], axis=0)
        phi = (own + jnp.dot(th_ref[case], halo, preferred_element_type=F32)).astype(BF16)
        psi = jnp.dot(phi, k_ref[...], preferred_element_type=F32)
        prod = phi.astype(F32) * psi
        prod = prod[:, :lanes] + prod[:, lanes:]
        high = prod.astype(BF16)
        low = (prod - high.astype(F32)).astype(BF16)
        dims = (((1,), (1,)), ((), ()))
        sums = lax.dot_general(ones, high, dims, preferred_element_type=F32)
        sums = sums + lax.dot_general(ones, low, dims, preferred_element_type=F32)
        cells = sums.shape[1]
        for j in range(cells // 128):
            row = n * (cells // 128) + j
            out_ref[row : row + 1] = sums[0:1, j * 128 : (j + 1) * 128]


def call(body, name, outs, args, scalars=0, scratch=(), flops=1e6, in_hbm=()):
    specs = [pl.BlockSpec(memory_space=pltpu.SMEM if i < scalars else pltpu.VMEM) for i in range(len(args))]
    args = [a if i < scalars else pltpu.with_memory_space_constraint(a, pltpu.VMEM) for i, a in enumerate(args)]
    size = sum(int(np.prod(o.shape)) * o.dtype.itemsize for o in outs)
    return pl.pallas_call(
        body,
        out_shape=tuple(outs),
        in_specs=specs,
        out_specs=tuple(pl.BlockSpec(memory_space=pltpu.VMEM) for _ in outs),
        scratch_shapes=list(scratch),
        name=name,
        compiler_params=pltpu.CompilerParams(vmem_limit_bytes=16 << 20),
        cost_estimate=pl.CostEstimate(flops=int(flops), bytes_accessed=size, transcendentals=0),
    )(*args)


def body(coefficients, fun_count, tile_offset, kernel, *, shape):
    bands, cx, cy, cz, slots = coefficients.shape
    text, mzh, th = make_tables(cy, cz)
    rows, cells, fx = cy * cz, 4 * cy * cz, 2 * cx
    near = [swap_pairs(shape, axis, True) for axis in range(3)]
    far = [swap_pairs(shape, axis, False) for axis in range(3)]
    send = lambda value, pairs: lax.ppermute(value, AXES, pairs)
    vmem = lambda shape, dtype: pltpu.VMEM(shape, dtype)
    count = fun_count.reshape(1)
    c = coefficients.reshape(bands, cx, rows, slots)
    face = vmem((4 * rows, slots), BF16)

    xnear, xfar = call(faces_kernel, "x_faces", [face] * 2, [count, c], 1)
    xnear, xfar = send(xnear, near[0]), send(xfar, far[0])
    own = kernel.reshape(kernel.shape[1:])
    tile1 = send(own, tile_pairs(shape))
    x, p, z = call(
        inner_kernel, "inner_cells",
        [vmem((fx - 2, 4 * rows, slots), BF16), vmem((fx - 2, cells, slots), F32), vmem((fx - 2, 4 * cy, slots), F32)],
        [count, c, text], 1, flops=2e9,
    )
    yshape = vmem((fx * 2 * cz, slots), BF16)
    edge, ynear, yfar = call(
        functools.partial(edge_kernel, cy=cy, cz=cz), "x_edges_y_faces",
        [vmem((2, 4 * rows, slots), BF16), yshape, yshape], [count, c, xnear, xfar, x], 1,
    )
    yfar, ynear = send(yfar, far[1]), send(ynear, near[1])
    tile2 = send(tile1, near[1])
    pe, ze = call(
        edge_cells_kernel, "edge_cells", [vmem((2, cells, slots), F32), vmem((2, 4 * cy, slots), F32)], [edge, text], flops=3e8
    )
    zshape = vmem((fx * 2 * cy, slots), BF16)
    znear, zfar = call(zfaces_kernel, "z_faces", [zshape, zshape], [ynear, yfar, z, ze, mzh])
    znear, zfar = send(znear, near[2]), send(zfar, far[2])
    (out,) = call(
        density_kernel, "density", [jax.ShapeDtypeStruct((fx * cells // 128, 128), F32)],
        [tile_offset.reshape(1), own, tile1, tile2, p, pe, th, ynear, yfar, znear, zfar], 1,
        scratch=[pltpu.VMEM((slots, slots), BF16)],
    )
    return out.reshape(1, 1, 1, -1)


def solution(mesh):
    placed = (
        P(None, "gx", "gy", "gz", None),
        P("gx", "gy", "gz"),
        P("gx", "gy", "gz"),
        P("gx", None, None),
    )
    shape = tuple(mesh.shape[a] for a in AXES)
    return jax.shard_map(
        functools.partial(body, shape=shape), mesh=mesh, in_specs=placed, out_specs=P("gx", "gy", "gz", None), check_vma=False
    )
```

```python
import functools

import jax
import jax.numpy as jnp
import ml_dtypes
import numpy as np
from jax import lax
from jax.experimental import pallas as pl
from jax.experimental.pallas import tpu as pltpu
from jax.sharding import PartitionSpec as P


FILT = [0.48296291314453416, 0.8365163037378079, 0.2241438680420134, -0.12940952255126037]
WAVE = [(1.0 if t % 2 == 0 else -1.0) * FILT[3 - t] for t in range(4)]
AXES = ("gx", "gy", "gz")
F32, BF16 = jnp.float32, jnp.bfloat16


def band_table(coarse):
    table = np.zeros((2, 2 * coarse, coarse))
    for fine in range(2 * coarse):
        for point in range(coarse):
            tap = fine - 2 * point + 1
            if 0 <= tap <= 3:
                table[0, fine, point] = FILT[tap]
                table[1, fine, point] = WAVE[tap]
    return table


def make_tables(cy, cz):
    ty, tz = band_table(cy), band_table(cz)
    fy, fz = 2 * cy, 2 * cz
    inner = np.einsum("cnk,dml->nmcdkl", ty, tz).reshape(fy, fz, 4 * cy * cz)
    zside = np.concatenate([inner[:, 0], inner[:, fz - 1]])
    inner = inner.reshape(fy * fz, 4 * cy * cz)
    ends = {}
    for name, plane, tap in (("first", 0, 0), ("last", cz - 1, 3)):
        pick = np.zeros((2, cz))
        pick[0, plane], pick[1, plane] = FILT[tap], WAVE[tap]
        own = np.einsum("cnk,dl->ncdkl", ty, pick).reshape(fy, 4 * cy * cz)
        before = np.zeros((fy, 2 * cz))
        before[0] = pick.reshape(-1)
        after = np.zeros((fy, 2 * cz))
        after[fy - 1] = pick.reshape(-1)
        ends[name] = (own, before, after)
    along = np.transpose(tz, (1, 0, 2)).reshape(fz, 2 * cz)
    adds = {}
    for name, row in (("before", 0), ("after", fy - 1)):
        rows = np.zeros((2, fz, 2 * cz))
        rows[0 if name == "before" else 1] = along
        sides = np.zeros((2, fy, 2 * cz))
        sides[0, row], sides[1, row] = along[0], along[fz - 1]
        adds[name] = np.concatenate([rows.reshape(2 * fz, -1), sides.reshape(2 * fy, -1)])
    text, mzh, add = [], [], []
    which = {"before": 1, "after": 2}
    for pz in range(2):
        order = ("last", "first") if pz == 0 else ("first", "last")
        text.append(np.concatenate([inner] + [ends[o][0] for o in order] + [zside]))
    for py in range(2):
        sides = ("after", "before") if py == 0 else ("before", "after")
        add.append(np.concatenate([adds[s] for s in sides], axis=1))
        for pz in range(2):
            order = ("last", "first") if pz == 0 else ("first", "last")
            mzh.append(np.concatenate([np.concatenate([ends[o][which[s]] for s in sides], axis=1) for o in order]))
    cast = lambda parts: np.stack(parts).astype(np.float32).astype(ml_dtypes.bfloat16)
    return cast(text), cast(mzh), cast(add)


def swap_pairs(shape, axis, near):
    out = []
    for place in np.ndindex(*shape):
        other = list(place)
        other[axis] = place[axis] ^ 1 if near else ((place[axis] - 1) ^ 1) + 1
        if 0 <= other[axis] < shape[axis]:
            out.append((int(np.ravel_multi_index(place, shape)), int(np.ravel_multi_index(other, shape))))
    return out


def tile_pairs(shape):
    nx, ny, _ = shape
    index = lambda x, y, z: int(np.ravel_multi_index((x % nx, y % ny, z), shape))
    out = []
    for x, y, z in np.ndindex(*shape):
        source = x - 1 if y % 2 == 0 else x + 1
        if source < nx:
            crosses = (source % nx) // 4 != x // 4
            out.append((index(source, y + 2 if crosses else y, z), index(x, y, z)))
    return out


def wrap_pairs(shape):
    nx, ny, nz = shape
    index = lambda x, y, z: int(np.ravel_multi_index((x, y, z), shape))
    return [(index(0, ny - y, z), index(nx - 1, y if y == 1 else ny - 1, z)) if y == 1 else (index(0, ny - 2, z), index(nx - 1, ny - 1, z)) for z in range(nz) for y in (1, 2)]


def last_pairs(shape):
    nx, ny, nz = shape
    index = lambda y, z: int(np.ravel_multi_index((nx - 1, y, z), shape))
    return [(index(y, z), index(y ^ 1, z)) for y in range(ny) for z in range(nz)]


def parity(axis):
    return lax.rem(lax.axis_index(axis), 2)


def lane_mask(count_ref, rows, lanes):
    return lax.broadcasted_iota(jnp.int32, (rows, lanes), 1) < count_ref[0]


def faces_kernel(count_ref, c_hbm, near_ref, far_ref, planes_ref, sem):
    last_k, rows = c_hbm.shape[1] - 1, c_hbm.shape[2]
    copies = [pltpu.make_async_copy(c_hbm.at[:, k], planes_ref.at[i], sem.at[i]) for i, k in enumerate((0, last_k))]
    for copy in copies:
        copy.start()
    even = parity("gx") == 0
    mask = lane_mask(count_ref, rows, c_hbm.shape[3])
    for copy in copies:
        copy.wait()
    for b in range(4):
        first = FILT[0] * planes_ref[0, b].astype(F32) + WAVE[0] * planes_ref[0, 4 + b].astype(F32)
        last = FILT[3] * planes_ref[1, b].astype(F32) + WAVE[3] * planes_ref[1, 4 + b].astype(F32)
        first, last = jnp.where(mask, first, 0.0), jnp.where(mask, last, 0.0)
        near_ref[b * rows : (b + 1) * rows] = jnp.where(even, last, first).astype(BF16)
        far_ref[b * rows : (b + 1) * rows] = jnp.where(even, first, last).astype(BF16)


def split_cells(r, i, mid_ref, yside_ref, z_ref, zside_ref):
    fz, sent = yside_ref.shape[1] // 2, z_ref.shape[1]
    cells = mid_ref.shape[1] + 2 * fz
    mid_ref[i] = r[fz : cells - fz].astype(BF16)
    yside_ref[i] = jnp.concatenate([r[:fz], r[cells - fz : cells]], axis=0)
    z_ref[i] = r[cells : cells + sent]
    zside_ref[i] = r[cells + sent :]


def inner_kernel(count_ref, c_hbm, text_ref, x_ref, mid_ref, yside_ref, z_ref, zside_ref, c_ref, sem):
    planes, rows = c_hbm.shape[1], c_hbm.shape[2]
    copies = [pltpu.make_async_copy(c_hbm.at[:, k], c_ref.at[k], sem.at[k]) for k in range(planes)]
    for copy in copies:
        copy.start()
    mask = lane_mask(count_ref, rows, c_hbm.shape[3])
    pz = parity("gz")
    copies[0].wait()
    for m in range(1, planes):
        copies[m].wait()
        odd, even = [], []
        for b in range(4):
            s0, w0 = c_ref[m - 1, b].astype(F32), c_ref[m - 1, 4 + b].astype(F32)
            s1, w1 = c_ref[m, b].astype(F32), c_ref[m, 4 + b].astype(F32)
            o = FILT[2] * s0 + WAVE[2] * w0 + FILT[0] * s1 + WAVE[0] * w1
            e = FILT[3] * s0 + WAVE[3] * w0 + FILT[1] * s1 + WAVE[1] * w1
            odd.append(jnp.where(mask, o, 0.0).astype(BF16))
            even.append(jnp.where(mask, e, 0.0).astype(BF16))
        for i, parts in ((2 * m - 2, odd), (2 * m - 1, even)):
            x = jnp.concatenate(parts, axis=0)
            x_ref[i] = x
            split_cells(jnp.dot(text_ref[pz], x, preferred_element_type=F32), i, mid_ref, yside_ref, z_ref, zside_ref)


def edge_kernel(count_ref, planes_ref, near_ref, far_ref, x_ref, edge_ref, ynear_ref, yfar_ref, *, cy, cz):
    rows = planes_ref.shape[2]
    mask = lane_mask(count_ref, rows, planes_ref.shape[3])
    even = parity("gx") == 0
    for b in range(4):
        near, far = near_ref[b * rows : (b + 1) * rows].astype(F32), far_ref[b * rows : (b + 1) * rows].astype(F32)
        before, after = jnp.where(even, far, near), jnp.where(even, near, far)
        s0, w0 = planes_ref[0, b].astype(F32), planes_ref[0, 4 + b].astype(F32)
        s1, w1 = planes_ref[1, b].astype(F32), planes_ref[1, 4 + b].astype(F32)
        lo = jnp.where(mask, FILT[1] * s0 + WAVE[1] * w0, 0.0) + before
        hi = jnp.where(mask, FILT[2] * s1 + WAVE[2] * w1, 0.0) + after
        edge_ref[0, b * rows : (b + 1) * rows] = lo.astype(BF16)
        edge_ref[1, b * rows : (b + 1) * rows] = hi.astype(BF16)
    even_y = parity("gy") == 0
    fine = x_ref.shape[0] + 2
    for n in range(fine):
        ref, i = (edge_ref, 0) if n == 0 else (edge_ref, 1) if n == fine - 1 else (x_ref, n - 1)
        near_rows, far_rows = [], []
        for zb in range(2):
            low, high = zb * rows, (2 + zb) * rows
            end = (cy - 1) * cz
            first = FILT[0] * ref[i, low : low + cz].astype(F32) + WAVE[0] * ref[i, high : high + cz].astype(F32)
            last = FILT[3] * ref[i, low + end : low + end + cz].astype(F32) + WAVE[3] * ref[i, high + end : high + end + cz].astype(F32)
            near_rows.append(jnp.where(even_y, last, first))
            far_rows.append(jnp.where(even_y, first, last))
        ynear_ref[n * 2 * cz : (n + 1) * 2 * cz] = jnp.concatenate(near_rows, axis=0).astype(BF16)
        yfar_ref[n * 2 * cz : (n + 1) * 2 * cz] = jnp.concatenate(far_rows, axis=0).astype(BF16)


def edge_cells_kernel(edge_ref, text_ref, *out_refs):
    pz = parity("gz")
    for i in range(2):
        split_cells(jnp.dot(text_ref[pz], edge_ref[i], preferred_element_type=F32), i, *out_refs)


def at(n, fine, inner_ref, edge_ref):
    return edge_ref[0] if n == 0 else edge_ref[1] if n == fine - 1 else inner_ref[n - 1]


def zfaces_kernel(ynear_ref, yfar_ref, z_ref, ze_ref, mzh_ref, near_ref, far_ref):
    case = 2 * parity("gy") + parity("gz")
    fine = z_ref.shape[0] + 2
    step = ynear_ref.shape[0] // fine
    half = z_ref.shape[1] // 2
    for n in range(fine):
        rows = slice(n * step, (n + 1) * step)
        halo = jnp.concatenate([ynear_ref[rows], yfar_ref[rows]], axis=0)
        r = at(n, fine, z_ref, ze_ref) + jnp.dot(mzh_ref[case], halo, preferred_element_type=F32)
        near_ref[n * half : (n + 1) * half] = r[:half].astype(BF16)
        far_ref[n * half : (n + 1) * half] = r[half:].astype(BF16)


def slot_sums(phi, k, wide):
    psi = jnp.dot(phi, k, preferred_element_type=F32)
    prod = phi.astype(F32) * psi
    half = prod.shape[1] // 2
    prod = prod[:, :half] + prod[:, half:]
    high = prod.astype(BF16)
    low = (prod - high.astype(F32)).astype(BF16)
    return jnp.dot(jnp.concatenate([high, low], axis=1), jnp.ones((2 * half, wide), BF16), preferred_element_type=F32)


def row_of(sums):
    lanes = sums.shape[1]
    diag = lax.broadcasted_iota(jnp.int32, (lanes, lanes), 0) == lax.broadcasted_iota(jnp.int32, (lanes, lanes), 1)
    parts = [jnp.where(diag, sums[i : i + lanes], 0.0) for i in range(0, sums.shape[0], lanes)]
    return jnp.concatenate([jnp.sum(part, axis=0, keepdims=True) for part in parts], axis=1)


def density_kernel(offset_ref, own_ref, tile1_ref, tile2_ref, ynear_ref, yfar_ref, add_ref, *rest):
    mid_ref, yside_ref, zside_ref, mide_ref, ysidee_ref, zsidee_ref, phi_ref, side_ref, d_ref, k_ref, own_out_ref = rest
    own_out_ref[...] = own_ref[...]
    even = parity("gy") == 0
    offset = offset_ref[0]
    first, second = tile1_ref[...], tile2_ref[...]
    before, after = jnp.where(even, first, second), jnp.where(even, second, first)
    k_ref[...] = jnp.where(offset == -1, before, jnp.where(offset == 1, after, own_ref[...]))
    fine = phi_ref.shape[0]
    step = ynear_ref.shape[0] // fine
    fz = yside_ref.shape[1] // 2
    for n in range(fine):
        rows = slice(n * step, (n + 1) * step)
        halo = jnp.concatenate([ynear_ref[rows], yfar_ref[rows]], axis=0)
        more = jnp.dot(add_ref[parity("gy")], halo, preferred_element_type=F32)
        ends = (at(n, fine, yside_ref, ysidee_ref) + more[: 2 * fz]).astype(BF16)
        side_ref[n] = at(n, fine, zside_ref, zsidee_ref) + more[2 * fz :]
        phi = jnp.concatenate([ends[:fz], at(n, fine, mid_ref, mide_ref), ends[fz:]], axis=0)
        phi_ref[n] = phi

    @pl.when(~in_last_domain())
    def _():
        for n in range(fine):
            d_ref[n : n + 1] = row_of(slot_sums(phi_ref[n], k_ref[...], 128))


def in_last_domain():
    return lax.axis_index("gx") == lax.axis_size("gx") - 1


def finish_kernel(offset_ref, wrap1_ref, wrap2_ref, near_ref, far_ref, phi_ref, side_ref, d_ref, k_ref, out_ref, tile_ref, dens_ref):
    fine, cells = d_ref.shape
    tile_ref[...] = k_ref[...]
    dens_ref[...] = d_ref[...]

    @pl.when(in_last_domain())
    def _():
        wrapped = jnp.where(parity("gy") == 0, wrap2_ref[...], wrap1_ref[...])
        tile_ref[...] = jnp.where(offset_ref[0] == 1, wrapped, k_ref[...])

        @pl.loop(0, fine)
        def _(n):
            dens_ref[pl.ds(n, 1)] = row_of(slot_sums(phi_ref[n], tile_ref[...], 128))

    even = parity("gz") == 0
    fy = near_ref.shape[0] // fine
    fz = cells // fy
    shape = (2 * fy, cells)
    row, lane = lax.broadcasted_iota(jnp.int32, shape, 0), lax.broadcasted_iota(jnp.int32, shape, 1)
    mine = lane == jnp.where(row < fy, row * fz, (row - fy) * fz + fz - 1)
    lane = lax.broadcasted_iota(jnp.int32, (1, cells), 1) % fz
    side = (lane == 0) | (lane == fz - 1)
    some = fine // 4
    for part in range(4):
        phi = []
        for n in range(part * some, (part + 1) * some):
            near, far = near_ref[n * fy : (n + 1) * fy].astype(F32), far_ref[n * fy : (n + 1) * fy].astype(F32)
            before, after = jnp.where(even, far, near), jnp.where(even, near, far)
            phi.append((side_ref[n] + jnp.concatenate([before, after], axis=0)).astype(BF16))
        sums = slot_sums(jnp.concatenate(phi, axis=0), tile_ref[...], cells)
        for i in range(some):
            n = part * some + i
            new = jnp.sum(jnp.where(mine, sums[i * 2 * fy : (i + 1) * 2 * fy], 0.0), axis=0, keepdims=True)
            new = jnp.where(side, new, dens_ref[n : n + 1])
            for j in range(cells // 128):
                out_ref[n * (cells // 128) + j : n * (cells // 128) + j + 1] = new[:, j * 128 : (j + 1) * 128]


def call(body, outs, args, scalars=0, scratch=(), flops=1e6, hbm=()):
    space = lambda i: pltpu.SMEM if i < scalars else pltpu.HBM if i in hbm else pltpu.VMEM
    specs = [pl.BlockSpec(memory_space=space(i)) for i in range(len(args))]
    args = [a if i < scalars else pltpu.with_memory_space_constraint(a, space(i)) for i, a in enumerate(args)]
    size = sum(int(np.prod(o.shape)) * o.dtype.itemsize for o in outs)
    return pl.pallas_call(
        body,
        out_shape=tuple(outs),
        in_specs=specs,
        out_specs=tuple(pl.BlockSpec(memory_space=pltpu.VMEM) for _ in outs),
        scratch_shapes=list(scratch),
        compiler_params=pltpu.CompilerParams(vmem_limit_bytes=16 << 20),
        cost_estimate=pl.CostEstimate(flops=int(flops), bytes_accessed=size, transcendentals=0),
    )(*args)


def send(value, pairs):
    return lax.ppermute(value, AXES, pairs)


def body(coefficients, fun_count, tile_offset, kernel, *, shape):
    return steps(coefficients, fun_count, tile_offset, kernel, shape)


def steps(coefficients, fun_count, tile_offset, kernel, shape):
    bands, cx, cy, cz, slots = coefficients.shape
    text, mzh, add = make_tables(cy, cz)
    rows, cells, fx = cy * cz, 4 * cy * cz, 2 * cx
    near = [swap_pairs(shape, axis, True) for axis in range(3)]
    far = [swap_pairs(shape, axis, False) for axis in range(3)]
    vmem = pltpu.VMEM
    count = fun_count.reshape(1)
    offset = tile_offset.reshape(1)
    c = coefficients.reshape(bands, cx, rows, slots)
    own = kernel.reshape(kernel.shape[1:])
    face = vmem((4 * rows, slots), BF16)

    xnear, xfar, planes = call(
        faces_kernel, [face, face, vmem((2, bands, rows, slots), BF16)], [count, c], 1,
        scratch=[pltpu.SemaphoreType.DMA((2,))], hbm=(1,),
    )
    xfar = send(xfar, far[0])
    xnear = send(xnear, near[0])
    tile1 = send(own, tile_pairs(shape))

    def cell_outs(n):
        return [
            vmem((n, cells - 4 * cz, slots), BF16), vmem((n, 4 * cz, slots), F32),
            vmem((n, 4 * cy, slots), F32), vmem((n, 4 * cy, slots), F32),
        ]

    x, mid, yside, z, zside = call(
        inner_kernel, [vmem((fx - 2, 4 * rows, slots), BF16)] + cell_outs(fx - 2), [count, c, text], 1,
        scratch=[vmem((cx, bands, rows, slots), BF16), pltpu.SemaphoreType.DMA((cx,))], flops=2e9, hbm=(1,),
    )
    yshape = vmem((fx * 2 * cz, slots), BF16)
    edge, ynear, yfar = call(
        functools.partial(edge_kernel, cy=cy, cz=cz),
        [vmem((2, 4 * rows, slots), BF16), yshape, yshape], [count, planes, xnear, xfar, x], 1,
    )
    yfar = send(yfar, far[1])
    ynear = send(ynear, near[1])
    mide, ysidee, ze, zsidee = call(edge_cells_kernel, cell_outs(2), [edge, text], flops=3e8)
    zshape = vmem((fx * 2 * cy, slots), BF16)
    znear, zfar = call(zfaces_kernel, [zshape, zshape], [ynear, yfar, z, ze, mzh])
    znear = send(znear, near[2])
    zfar = send(zfar, far[2])
    tile2 = send(tile1, near[1])
    square = vmem((slots, slots), BF16)
    phi, side, d, tile, own_late = call(
        density_kernel,
        [vmem((fx, cells, slots), BF16), vmem((fx, 4 * cy, slots), F32), vmem((fx, cells), F32), square, square],
        [offset, own, tile1, tile2, ynear, yfar, add, mid, yside, zside, mide, ysidee, zsidee], 1, flops=2e9,
    )
    wrap1 = send(own_late, wrap_pairs(shape))
    wrap2 = send(wrap1, last_pairs(shape))
    (out,) = call(
        finish_kernel, [jax.ShapeDtypeStruct((fx * cells // 128, 128), F32)],
        [offset, wrap1, wrap2, znear, zfar, phi, side, d, tile], 1,
        scratch=[vmem((slots, slots), BF16), vmem((fx, cells), F32)],
    )
    return out.reshape(1, 1, 1, -1)


def solution(mesh):
    placed = (
        P(None, "gx", "gy", "gz", None),
        P("gx", "gy", "gz"),
        P("gx", "gy", "gz"),
        P("gx", None, None),
    )
    shape = tuple(mesh.shape[a] for a in AXES)
    return jax.shard_map(
        functools.partial(body, shape=shape), mesh=mesh, in_specs=placed, out_specs=P("gx", "gy", "gz", None), check_vma=False
    )
```

```python
import functools

import jax
import jax.numpy as jnp
import ml_dtypes
import numpy as np
from jax import lax
from jax.experimental import pallas as pl
from jax.experimental.pallas import tpu as pltpu
from jax.sharding import PartitionSpec as P


FILT = [0.48296291314453416, 0.8365163037378079, 0.2241438680420134, -0.12940952255126037]
WAVE = [(1.0 if t % 2 == 0 else -1.0) * FILT[3 - t] for t in range(4)]
AXES = ("gx", "gy", "gz")
F32, BF16 = jnp.float32, jnp.bfloat16


def band_table(coarse):
    table = np.zeros((2, 2 * coarse, coarse))
    for fine in range(2 * coarse):
        for point in range(coarse):
            tap = fine - 2 * point + 1
            if 0 <= tap <= 3:
                table[0, fine, point] = FILT[tap]
                table[1, fine, point] = WAVE[tap]
    return table


def make_tables(cy, cz):
    ty, tz = band_table(cy), band_table(cz)
    fy, fz = 2 * cy, 2 * cz
    inner = np.einsum("cnk,dml->nmcdkl", ty, tz).reshape(fy, fz, 4 * cy * cz)
    zside = np.concatenate([inner[:, 0], inner[:, fz - 1]])
    inner = inner.reshape(fy * fz, 4 * cy * cz)
    ends = {}
    for name, plane, tap in (("first", 0, 0), ("last", cz - 1, 3)):
        pick = np.zeros((2, cz))
        pick[0, plane], pick[1, plane] = FILT[tap], WAVE[tap]
        own = np.einsum("cnk,dl->ncdkl", ty, pick).reshape(fy, 4 * cy * cz)
        before = np.zeros((fy, 2 * cz))
        before[0] = pick.reshape(-1)
        after = np.zeros((fy, 2 * cz))
        after[fy - 1] = pick.reshape(-1)
        ends[name] = (own, before, after)
    along = np.transpose(tz, (1, 0, 2)).reshape(fz, 2 * cz)
    adds = {}
    for name, row in (("before", 0), ("after", fy - 1)):
        rows = np.zeros((2, fz, 2 * cz))
        rows[0 if name == "before" else 1] = along
        sides = np.zeros((2, fy, 2 * cz))
        sides[0, row], sides[1, row] = along[0], along[fz - 1]
        adds[name] = np.concatenate([rows.reshape(2 * fz, -1), sides.reshape(2 * fy, -1)])
    text, mzh, add = [], [], []
    which = {"before": 1, "after": 2}
    for pz in range(2):
        order = ("last", "first") if pz == 0 else ("first", "last")
        text.append(np.concatenate([inner] + [ends[o][0] for o in order] + [zside]))
    for py in range(2):
        sides = ("after", "before") if py == 0 else ("before", "after")
        add.append(np.concatenate([adds[s] for s in sides], axis=1))
        for pz in range(2):
            order = ("last", "first") if pz == 0 else ("first", "last")
            mzh.append(np.concatenate([np.concatenate([ends[o][which[s]] for s in sides], axis=1) for o in order]))
    cast = lambda parts: np.stack(parts).astype(np.float32).astype(ml_dtypes.bfloat16)
    return cast(text), cast(mzh), cast(add)


def swap_pairs(shape, axis, near):
    out = []
    for place in np.ndindex(*shape):
        other = list(place)
        other[axis] = place[axis] ^ 1 if near else ((place[axis] - 1) ^ 1) + 1
        if 0 <= other[axis] < shape[axis]:
            out.append((int(np.ravel_multi_index(place, shape)), int(np.ravel_multi_index(other, shape))))
    return out


def tile_pairs(shape):
    nx, ny, _ = shape
    index = lambda x, y, z: int(np.ravel_multi_index((x % nx, y % ny, z), shape))
    out = []
    for x, y, z in np.ndindex(*shape):
        source = x - 1 if y % 2 == 0 else x + 1
        if source < nx:
            crosses = (source % nx) // 4 != x // 4
            out.append((index(source, y + 2 if crosses else y, z), index(x, y, z)))
    return out


def wrap_pairs(shape):
    nx, ny, nz = shape
    index = lambda x, y, z: int(np.ravel_multi_index((x, y, z), shape))
    return [(index(0, ny - 2 + y, z), index(nx - 1, y, z)) for y in range(2) for z in range(nz)]


def last_pairs(shape):
    nx, ny, nz = shape
    index = lambda y, z: int(np.ravel_multi_index((nx - 1, y, z), shape))
    return [(index(y, z), index(y + ny - 2, z)) for y in range(2) for z in range(nz)]


def parity(axis):
    return lax.rem(lax.axis_index(axis), 2)


def lane_mask(count_ref, rows, lanes):
    return lax.broadcasted_iota(jnp.int32, (rows, lanes), 1) < count_ref[0]


def faces_kernel(count_ref, c_hbm, text_hbm, near_ref, far_ref, planes_ref, text_ref, sem):
    last_k, rows = c_hbm.shape[1] - 1, c_hbm.shape[2]
    copies = [pltpu.make_async_copy(c_hbm.at[:, k], planes_ref.at[i], sem.at[i]) for i, k in enumerate((0, last_k))]
    table = pltpu.make_async_copy(text_hbm.at[parity("gz")], text_ref, sem.at[2])
    for copy in copies:
        copy.start()
    table.start()
    even = parity("gx") == 0
    mask = lane_mask(count_ref, rows, c_hbm.shape[3])
    for copy in copies:
        copy.wait()
    for b in range(4):
        first = FILT[0] * planes_ref[0, b].astype(F32) + WAVE[0] * planes_ref[0, 4 + b].astype(F32)
        last = FILT[3] * planes_ref[1, b].astype(F32) + WAVE[3] * planes_ref[1, 4 + b].astype(F32)
        first, last = jnp.where(mask, first, 0.0), jnp.where(mask, last, 0.0)
        near_ref[b * rows : (b + 1) * rows] = jnp.where(even, last, first).astype(BF16)
        far_ref[b * rows : (b + 1) * rows] = jnp.where(even, first, last).astype(BF16)
    table.wait()


def split_cells(r, i, mid_ref, yside_ref, z_ref, zside_ref):
    fz, sent = yside_ref.shape[1] // 2, z_ref.shape[1]
    cells = mid_ref.shape[1] + 2 * fz
    mid_ref[i] = r[fz : cells - fz].astype(BF16)
    yside_ref[i] = jnp.concatenate([r[:fz], r[cells - fz : cells]], axis=0)
    z_ref[i] = r[cells : cells + sent]
    zside_ref[i] = r[cells + sent :]


def inner_kernel(count_ref, c_ref, text_ref, x_ref, mid_ref, yside_ref, z_ref, zside_ref):
    planes, rows = c_ref.shape[1], c_ref.shape[2]
    mask = lane_mask(count_ref, rows, c_ref.shape[3])
    for m in range(1, planes):
        odd, even = [], []
        for b in range(4):
            s0, w0 = c_ref[b, m - 1].astype(F32), c_ref[4 + b, m - 1].astype(F32)
            s1, w1 = c_ref[b, m].astype(F32), c_ref[4 + b, m].astype(F32)
            o = FILT[2] * s0 + WAVE[2] * w0 + FILT[0] * s1 + WAVE[0] * w1
            e = FILT[3] * s0 + WAVE[3] * w0 + FILT[1] * s1 + WAVE[1] * w1
            odd.append(jnp.where(mask, o, 0.0).astype(BF16))
            even.append(jnp.where(mask, e, 0.0).astype(BF16))
        for i, parts in ((2 * m - 2, odd), (2 * m - 1, even)):
            x = jnp.concatenate(parts, axis=0)
            x_ref[i] = x
            split_cells(jnp.dot(text_ref[...], x, preferred_element_type=F32), i, mid_ref, yside_ref, z_ref, zside_ref)


def edge_kernel(count_ref, planes_ref, near_ref, far_ref, x_ref, edge_ref, ynear_ref, yfar_ref, *, cy, cz):
    rows = planes_ref.shape[2]
    mask = lane_mask(count_ref, rows, planes_ref.shape[3])
    even = parity("gx") == 0
    for b in range(4):
        near, far = near_ref[b * rows : (b + 1) * rows].astype(F32), far_ref[b * rows : (b + 1) * rows].astype(F32)
        before, after = jnp.where(even, far, near), jnp.where(even, near, far)
        s0, w0 = planes_ref[0, b].astype(F32), planes_ref[0, 4 + b].astype(F32)
        s1, w1 = planes_ref[1, b].astype(F32), planes_ref[1, 4 + b].astype(F32)
        lo = jnp.where(mask, FILT[1] * s0 + WAVE[1] * w0, 0.0) + before
        hi = jnp.where(mask, FILT[2] * s1 + WAVE[2] * w1, 0.0) + after
        edge_ref[0, b * rows : (b + 1) * rows] = lo.astype(BF16)
        edge_ref[1, b * rows : (b + 1) * rows] = hi.astype(BF16)
    even_y = parity("gy") == 0
    fine = x_ref.shape[0] + 2
    for n in range(fine):
        ref, i = (edge_ref, 0) if n == 0 else (edge_ref, 1) if n == fine - 1 else (x_ref, n - 1)
        near_rows, far_rows = [], []
        for zb in range(2):
            low, high = zb * rows, (2 + zb) * rows
            end = (cy - 1) * cz
            first = FILT[0] * ref[i, low : low + cz].astype(F32) + WAVE[0] * ref[i, high : high + cz].astype(F32)
            last = FILT[3] * ref[i, low + end : low + end + cz].astype(F32) + WAVE[3] * ref[i, high + end : high + end + cz].astype(F32)
            near_rows.append(jnp.where(even_y, last, first))
            far_rows.append(jnp.where(even_y, first, last))
        ynear_ref[n * 2 * cz : (n + 1) * 2 * cz] = jnp.concatenate(near_rows, axis=0).astype(BF16)
        yfar_ref[n * 2 * cz : (n + 1) * 2 * cz] = jnp.concatenate(far_rows, axis=0).astype(BF16)


def edge_cells_kernel(edge_ref, text_ref, *out_refs):
    for i in range(2):
        split_cells(jnp.dot(text_ref[...], edge_ref[i], preferred_element_type=F32), i, *out_refs)


def at(n, fine, inner_ref, edge_ref):
    return edge_ref[0] if n == 0 else edge_ref[1] if n == fine - 1 else inner_ref[n - 1]


def zfaces_kernel(ynear_ref, yfar_ref, z_ref, ze_ref, mzh_ref, near_ref, far_ref):
    case = 2 * parity("gy") + parity("gz")
    fine = z_ref.shape[0] + 2
    step = ynear_ref.shape[0] // fine
    half = z_ref.shape[1] // 2
    for n in range(fine):
        rows = slice(n * step, (n + 1) * step)
        halo = jnp.concatenate([ynear_ref[rows], yfar_ref[rows]], axis=0)
        r = at(n, fine, z_ref, ze_ref) + jnp.dot(mzh_ref[case], halo, preferred_element_type=F32)
        near_ref[n * half : (n + 1) * half] = r[:half].astype(BF16)
        far_ref[n * half : (n + 1) * half] = r[half:].astype(BF16)


def slot_sums(phi, k, wide):
    psi = jnp.dot(phi, k, preferred_element_type=F32)
    prod = phi.astype(F32) * psi
    half = prod.shape[1] // 2
    prod = prod[:, :half] + prod[:, half:]
    high = prod.astype(BF16)
    low = (prod - high.astype(F32)).astype(BF16)
    return jnp.dot(jnp.concatenate([high, low], axis=1), jnp.ones((2 * half, wide), BF16), preferred_element_type=F32)


def row_of(sums):
    lanes = sums.shape[1]
    diag = lax.broadcasted_iota(jnp.int32, (lanes, lanes), 0) == lax.broadcasted_iota(jnp.int32, (lanes, lanes), 1)
    parts = [jnp.where(diag, sums[i : i + lanes], 0.0) for i in range(0, sums.shape[0], lanes)]
    return jnp.concatenate([jnp.sum(part, axis=0, keepdims=True) for part in parts], axis=1)


def density_kernel(offset_ref, own_ref, tile1_ref, tile2_ref, wrap1_ref, wrap2_ref, ynear_ref, yfar_ref, add_ref, *rest):
    mid_ref, yside_ref, zside_ref, mide_ref, ysidee_ref, zsidee_ref, side_ref, d_ref, k_ref = rest
    even = parity("gy") == 0
    offset = offset_ref[0]
    first, second = tile1_ref[...], tile2_ref[...]
    before, after = jnp.where(even, first, second), jnp.where(even, second, first)
    wrapped = jnp.where(lax.axis_index("gy") < 2, wrap1_ref[...], wrap2_ref[...])
    after = jnp.where(lax.axis_index("gx") == lax.axis_size("gx") - 1, wrapped, after)
    k_ref[...] = jnp.where(offset == -1, before, jnp.where(offset == 1, after, own_ref[...]))
    fine = d_ref.shape[0]
    step = ynear_ref.shape[0] // fine
    fz = yside_ref.shape[1] // 2
    for n in range(fine):
        rows = slice(n * step, (n + 1) * step)
        halo = jnp.concatenate([ynear_ref[rows], yfar_ref[rows]], axis=0)
        more = jnp.dot(add_ref[parity("gy")], halo, preferred_element_type=F32)
        ends = (at(n, fine, yside_ref, ysidee_ref) + more[: 2 * fz]).astype(BF16)
        side_ref[n] = at(n, fine, zside_ref, zsidee_ref) + more[2 * fz :]
        phi = jnp.concatenate([ends[:fz], at(n, fine, mid_ref, mide_ref), ends[fz:]], axis=0)
        d_ref[n : n + 1] = row_of(slot_sums(phi, k_ref[...], 128))


def finish_kernel(near_ref, far_ref, side_ref, d_ref, tile_ref, out_ref):
    fine, cells = d_ref.shape
    even = parity("gz") == 0
    fy = near_ref.shape[0] // fine
    fz = cells // fy
    shape = (2 * fy, cells)
    row, lane = lax.broadcasted_iota(jnp.int32, shape, 0), lax.broadcasted_iota(jnp.int32, shape, 1)
    mine = lane == jnp.where(row < fy, row * fz, (row - fy) * fz + fz - 1)
    lane = lax.broadcasted_iota(jnp.int32, (1, cells), 1) % fz
    side = (lane == 0) | (lane == fz - 1)
    some = fine // 4
    for part in range(4):
        phi = []
        for n in range(part * some, (part + 1) * some):
            near, far = near_ref[n * fy : (n + 1) * fy].astype(F32), far_ref[n * fy : (n + 1) * fy].astype(F32)
            before, after = jnp.where(even, far, near), jnp.where(even, near, far)
            phi.append((side_ref[n] + jnp.concatenate([before, after], axis=0)).astype(BF16))
        sums = slot_sums(jnp.concatenate(phi, axis=0), tile_ref[...], cells)
        for i in range(some):
            n = part * some + i
            new = jnp.sum(jnp.where(mine, sums[i * 2 * fy : (i + 1) * 2 * fy], 0.0), axis=0, keepdims=True)
            new = jnp.where(side, new, d_ref[n : n + 1])
            for j in range(cells // 128):
                out_ref[n * (cells // 128) + j : n * (cells // 128) + j + 1] = new[:, j * 128 : (j + 1) * 128]


def call(body, outs, args, scalars=0, scratch=(), flops=1e6, hbm=()):
    space = lambda i: pltpu.SMEM if i < scalars else pltpu.HBM if i in hbm else pltpu.VMEM
    specs = [pl.BlockSpec(memory_space=space(i)) for i in range(len(args))]
    args = [a if i < scalars else pltpu.with_memory_space_constraint(a, space(i)) for i, a in enumerate(args)]
    size = sum(int(np.prod(o.shape)) * o.dtype.itemsize for o in outs)
    return pl.pallas_call(
        body,
        out_shape=tuple(outs),
        in_specs=specs,
        out_specs=tuple(pl.BlockSpec(memory_space=pltpu.VMEM) for _ in outs),
        scratch_shapes=list(scratch),
        compiler_params=pltpu.CompilerParams(vmem_limit_bytes=16 << 20),
        cost_estimate=pl.CostEstimate(flops=int(flops), bytes_accessed=size, transcendentals=0),
    )(*args)


def send(value, pairs):
    return lax.ppermute(value, AXES, pairs)


def body(coefficients, fun_count, tile_offset, kernel, *, shape):
    return steps(coefficients, fun_count, tile_offset, kernel, shape)


def steps(coefficients, fun_count, tile_offset, kernel, shape):
    bands, cx, cy, cz, slots = coefficients.shape
    text, mzh, add = make_tables(cy, cz)
    rows, cells, fx = cy * cz, 4 * cy * cz, 2 * cx
    near = [swap_pairs(shape, axis, True) for axis in range(3)]
    far = [swap_pairs(shape, axis, False) for axis in range(3)]
    vmem = pltpu.VMEM
    count = fun_count.reshape(1)
    offset = tile_offset.reshape(1)
    c = coefficients.reshape(bands, cx, rows, slots)
    own = kernel.reshape(kernel.shape[1:])
    face = vmem((4 * rows, slots), BF16)

    xnear, xfar, planes, text = call(
        faces_kernel, [face, face, vmem((2, bands, rows, slots), BF16), vmem(text.shape[1:], BF16)], [count, c, text], 1,
        scratch=[pltpu.SemaphoreType.DMA((3,))], hbm=(1, 2),
    )
    xfar = send(xfar, far[0])
    xnear = send(xnear, near[0])
    tile1 = send(own, tile_pairs(shape))

    def cell_outs(n):
        return [
            vmem((n, cells - 4 * cz, slots), BF16), vmem((n, 4 * cz, slots), F32),
            vmem((n, 4 * cy, slots), F32), vmem((n, 4 * cy, slots), F32),
        ]

    x, mid, yside, z, zside = call(
        inner_kernel, [vmem((fx - 2, 4 * rows, slots), BF16)] + cell_outs(fx - 2), [count, c, text], 1,
        flops=2e9,
    )
    yshape = vmem((fx * 2 * cz, slots), BF16)
    edge, ynear, yfar = call(
        functools.partial(edge_kernel, cy=cy, cz=cz),
        [vmem((2, 4 * rows, slots), BF16), yshape, yshape], [count, planes, xnear, xfar, x], 1,
    )
    yfar = send(yfar, far[1])
    ynear = send(ynear, near[1])
    wrap1 = send(own, wrap_pairs(shape))
    mide, ysidee, ze, zsidee = call(edge_cells_kernel, cell_outs(2), [edge, text], flops=3e8)
    zshape = vmem((fx * 2 * cy, slots), BF16)
    znear, zfar = call(zfaces_kernel, [zshape, zshape], [ynear, yfar, z, ze, mzh])
    znear = send(znear, near[2])
    zfar = send(zfar, far[2])
    tile2 = send(tile1, near[1])
    wrap2 = send(wrap1, last_pairs(shape))
    side, d, tile = call(
        density_kernel, [vmem((fx, 4 * cy, slots), F32), vmem((fx, cells), F32), vmem((slots, slots), BF16)],
        [offset, own, tile1, tile2, wrap1, wrap2, ynear, yfar, add, mid, yside, zside, mide, ysidee, zsidee], 1, flops=2e9,
    )
    (out,) = call(finish_kernel, [jax.ShapeDtypeStruct((fx * cells // 128, 128), F32)], [znear, zfar, side, d, tile])
    return out.reshape(1, 1, 1, -1)


def solution(mesh):
    placed = (
        P(None, "gx", "gy", "gz", None),
        P("gx", "gy", "gz"),
        P("gx", "gy", "gz"),
        P("gx", None, None),
    )
    shape = tuple(mesh.shape[a] for a in AXES)
    return jax.shard_map(
        functools.partial(body, shape=shape), mesh=mesh, in_specs=placed, out_specs=P("gx", "gy", "gz", None), check_vma=False
    )
```

```python
import functools

import jax
import jax.numpy as jnp
import ml_dtypes
import numpy as np
from jax import lax
from jax.experimental import pallas as pl
from jax.experimental.pallas import tpu as pltpu
from jax.sharding import PartitionSpec as P


FILT = [0.48296291314453416, 0.8365163037378079, 0.2241438680420134, -0.12940952255126037]
WAVE = [(1.0 if t % 2 == 0 else -1.0) * FILT[3 - t] for t in range(4)]
AXES = ("gx", "gy", "gz")
F32, BF16 = jnp.float32, jnp.bfloat16


def band_table(coarse):
    table = np.zeros((2, 2 * coarse, coarse))
    for fine in range(2 * coarse):
        for point in range(coarse):
            tap = fine - 2 * point + 1
            if 0 <= tap <= 3:
                table[0, fine, point] = FILT[tap]
                table[1, fine, point] = WAVE[tap]
    return table


def make_tables(cy, cz):
    ty, tz = band_table(cy), band_table(cz)
    fy, fz = 2 * cy, 2 * cz
    inner = np.einsum("cnk,dml->nmcdkl", ty, tz).reshape(fy, fz, 4 * cy * cz)
    zside = np.concatenate([inner[:, 0], inner[:, fz - 1]])
    inner = inner.reshape(fy * fz, 4 * cy * cz)
    ends = {}
    for name, plane, tap in (("first", 0, 0), ("last", cz - 1, 3)):
        pick = np.zeros((2, cz))
        pick[0, plane], pick[1, plane] = FILT[tap], WAVE[tap]
        own = np.einsum("cnk,dl->ncdkl", ty, pick).reshape(fy, 4 * cy * cz)
        before = np.zeros((fy, 2 * cz))
        before[0] = pick.reshape(-1)
        after = np.zeros((fy, 2 * cz))
        after[fy - 1] = pick.reshape(-1)
        ends[name] = (own, before, after)
    along = np.transpose(tz, (1, 0, 2)).reshape(fz, 2 * cz)
    adds = {}
    for name, row in (("before", 0), ("after", fy - 1)):
        rows = np.zeros((2, fz, 2 * cz))
        rows[0 if name == "before" else 1] = along
        sides = np.zeros((2, fy, 2 * cz))
        sides[0, row], sides[1, row] = along[0], along[fz - 1]
        adds[name] = np.concatenate([rows.reshape(2 * fz, -1), sides.reshape(2 * fy, -1)])
    text, mzh, add = [], [], []
    which = {"before": 1, "after": 2}
    for pz in range(2):
        order = ("last", "first") if pz == 0 else ("first", "last")
        text.append(np.concatenate([inner] + [ends[o][0] for o in order] + [zside]))
    for py in range(2):
        sides = ("after", "before") if py == 0 else ("before", "after")
        add.append(np.concatenate([adds[s] for s in sides], axis=1))
        for pz in range(2):
            order = ("last", "first") if pz == 0 else ("first", "last")
            mzh.append(np.concatenate([np.concatenate([ends[o][which[s]] for s in sides], axis=1) for o in order]))
    cast = lambda parts: np.stack(parts).astype(np.float32).astype(ml_dtypes.bfloat16)
    return cast(text), cast(mzh), cast(add)


def swap_pairs(shape, axis, near):
    out = []
    for place in np.ndindex(*shape):
        other = list(place)
        other[axis] = place[axis] ^ 1 if near else ((place[axis] - 1) ^ 1) + 1
        if 0 <= other[axis] < shape[axis]:
            out.append((int(np.ravel_multi_index(place, shape)), int(np.ravel_multi_index(other, shape))))
    return out


def tile_pairs(shape):
    nx, ny, _ = shape
    out = []
    for x, y, z in np.ndindex(*shape):
        source = x - 1 if y % 2 == 0 else x + 1
        if 0 <= source < nx:
            place = (source, (y + ny // 2) % ny if source // 4 != x // 4 else y, z)
            out.append((at_place(shape, *place), at_place(shape, x, y, z)))
    return out


def at_place(shape, x, y, z):
    return int(np.ravel_multi_index((x, y, z), shape))


def round_pairs(shape):
    nx, ny, nz = shape
    up, down1, down2 = [], [], []
    stops = ((3, 15, 1, 1), (2, 12, 3, 3))
    for z in range(nz):
        for y in (0, 2):
            up.append((at_place(shape, nx - 1, (y + 2) % ny, z), at_place(shape, 0, y, z)))
        for y, stop_x, stop_y, last_y in stops:
            down1.append((at_place(shape, 0, y, z), at_place(shape, stop_x, stop_y, z)))
            down2.append((at_place(shape, stop_x, stop_y, z), at_place(shape, nx - 1, last_y, z)))
    return up, down1, down2


def parity(axis):
    return lax.rem(lax.axis_index(axis), 2)


def lane_mask(count_ref, rows, lanes):
    return lax.broadcasted_iota(jnp.int32, (rows, lanes), 1) < count_ref[0]


def faces_kernel(count_ref, c_hbm, text_hbm, near_ref, far_ref, planes_ref, text_ref, sem):
    last_k, rows = c_hbm.shape[1] - 1, c_hbm.shape[2]
    copies = [pltpu.make_async_copy(c_hbm.at[:, k], planes_ref.at[i], sem.at[i]) for i, k in enumerate((0, last_k))]
    table = pltpu.make_async_copy(text_hbm.at[parity("gz")], text_ref, sem.at[2])
    for copy in copies:
        copy.start()
    table.start()
    even = parity("gx") == 0
    mask = lane_mask(count_ref, rows, c_hbm.shape[3])
    for copy in copies:
        copy.wait()
    for b in range(4):
        first = FILT[0] * planes_ref[0, b].astype(F32) + WAVE[0] * planes_ref[0, 4 + b].astype(F32)
        last = FILT[3] * planes_ref[1, b].astype(F32) + WAVE[3] * planes_ref[1, 4 + b].astype(F32)
        first, last = jnp.where(mask, first, 0.0), jnp.where(mask, last, 0.0)
        near_ref[b * rows : (b + 1) * rows] = jnp.where(even, last, first).astype(BF16)
        far_ref[b * rows : (b + 1) * rows] = jnp.where(even, first, last).astype(BF16)
    table.wait()


def split_cells(r, i, mid_ref, yside_ref, z_ref, zside_ref):
    fz, sent = yside_ref.shape[1] // 2, z_ref.shape[1]
    cells = mid_ref.shape[1] + 2 * fz
    mid_ref[i] = r[fz : cells - fz].astype(BF16)
    yside_ref[i] = jnp.concatenate([r[:fz], r[cells - fz : cells]], axis=0)
    z_ref[i] = r[cells : cells + sent]
    zside_ref[i] = r[cells + sent :]


def inner_kernel(count_ref, c_ref, text_ref, x_ref, mid_ref, yside_ref, z_ref, zside_ref):
    planes, rows = c_ref.shape[1], c_ref.shape[2]
    mask = lane_mask(count_ref, rows, c_ref.shape[3])
    for m in range(1, planes):
        odd, even = [], []
        for b in range(4):
            s0, w0 = c_ref[b, m - 1].astype(F32), c_ref[4 + b, m - 1].astype(F32)
            s1, w1 = c_ref[b, m].astype(F32), c_ref[4 + b, m].astype(F32)
            o = FILT[2] * s0 + WAVE[2] * w0 + FILT[0] * s1 + WAVE[0] * w1
            e = FILT[3] * s0 + WAVE[3] * w0 + FILT[1] * s1 + WAVE[1] * w1
            odd.append(jnp.where(mask, o, 0.0).astype(BF16))
            even.append(jnp.where(mask, e, 0.0).astype(BF16))
        for i, parts in ((2 * m - 2, odd), (2 * m - 1, even)):
            x = jnp.concatenate(parts, axis=0)
            x_ref[i] = x
            split_cells(jnp.dot(text_ref[...], x, preferred_element_type=F32), i, mid_ref, yside_ref, z_ref, zside_ref)


def edge_kernel(count_ref, planes_ref, near_ref, far_ref, x_ref, edge_ref, ynear_ref, yfar_ref, *, cy, cz):
    rows = planes_ref.shape[2]
    mask = lane_mask(count_ref, rows, planes_ref.shape[3])
    even = parity("gx") == 0
    for b in range(4):
        near, far = near_ref[b * rows : (b + 1) * rows].astype(F32), far_ref[b * rows : (b + 1) * rows].astype(F32)
        before, after = jnp.where(even, far, near), jnp.where(even, near, far)
        s0, w0 = planes_ref[0, b].astype(F32), planes_ref[0, 4 + b].astype(F32)
        s1, w1 = planes_ref[1, b].astype(F32), planes_ref[1, 4 + b].astype(F32)
        lo = jnp.where(mask, FILT[1] * s0 + WAVE[1] * w0, 0.0) + before
        hi = jnp.where(mask, FILT[2] * s1 + WAVE[2] * w1, 0.0) + after
        edge_ref[0, b * rows : (b + 1) * rows] = lo.astype(BF16)
        edge_ref[1, b * rows : (b + 1) * rows] = hi.astype(BF16)
    even_y = parity("gy") == 0
    fine = x_ref.shape[0] + 2
    for n in range(fine):
        ref, i = (edge_ref, 0) if n == 0 else (edge_ref, 1) if n == fine - 1 else (x_ref, n - 1)
        near_rows, far_rows = [], []
        for zb in range(2):
            low, high = zb * rows, (2 + zb) * rows
            end = (cy - 1) * cz
            first = FILT[0] * ref[i, low : low + cz].astype(F32) + WAVE[0] * ref[i, high : high + cz].astype(F32)
            last = FILT[3] * ref[i, low + end : low + end + cz].astype(F32) + WAVE[3] * ref[i, high + end : high + end + cz].astype(F32)
            near_rows.append(jnp.where(even_y, last, first))
            far_rows.append(jnp.where(even_y, first, last))
        ynear_ref[n * 2 * cz : (n + 1) * 2 * cz] = jnp.concatenate(near_rows, axis=0).astype(BF16)
        yfar_ref[n * 2 * cz : (n + 1) * 2 * cz] = jnp.concatenate(far_rows, axis=0).astype(BF16)


def edge_cells_kernel(edge_ref, text_ref, *out_refs):
    for i in range(2):
        split_cells(jnp.dot(text_ref[...], edge_ref[i], preferred_element_type=F32), i, *out_refs)


def at(n, fine, inner_ref, edge_ref):
    return edge_ref[0] if n == 0 else edge_ref[1] if n == fine - 1 else inner_ref[n - 1]


def zfaces_kernel(ynear_ref, yfar_ref, z_ref, ze_ref, mzh_ref, near_ref, far_ref):
    case = 2 * parity("gy") + parity("gz")
    fine = z_ref.shape[0] + 2
    step = ynear_ref.shape[0] // fine
    half = z_ref.shape[1] // 2
    for n in range(fine):
        rows = slice(n * step, (n + 1) * step)
        halo = jnp.concatenate([ynear_ref[rows], yfar_ref[rows]], axis=0)
        r = at(n, fine, z_ref, ze_ref) + jnp.dot(mzh_ref[case], halo, preferred_element_type=F32)
        near_ref[n * half : (n + 1) * half] = r[:half].astype(BF16)
        far_ref[n * half : (n + 1) * half] = r[half:].astype(BF16)


def slot_sums(phi, k, wide):
    psi = jnp.dot(phi, k, preferred_element_type=F32)
    prod = phi.astype(F32) * psi
    half = prod.shape[1] // 2
    prod = prod[:, :half] + prod[:, half:]
    high = prod.astype(BF16)
    low = (prod - high.astype(F32)).astype(BF16)
    return jnp.dot(jnp.concatenate([high, low], axis=1), jnp.ones((2 * half, wide), BF16), preferred_element_type=F32)


def row_of(sums):
    lanes = sums.shape[1]
    diag = lax.broadcasted_iota(jnp.int32, (lanes, lanes), 0) == lax.broadcasted_iota(jnp.int32, (lanes, lanes), 1)
    parts = [jnp.where(diag, sums[i : i + lanes], 0.0) for i in range(0, sums.shape[0], lanes)]
    return jnp.concatenate([jnp.sum(part, axis=0, keepdims=True) for part in parts], axis=1)


def density_kernel(offset_ref, own_ref, tile1_ref, tile2_ref, ynear_ref, yfar_ref, add_ref, *rest):
    mid_ref, yside_ref, zside_ref, mide_ref, ysidee_ref, zsidee_ref, side_ref, d_ref, k_ref, phi_ref = rest
    even = parity("gy") == 0
    offset = offset_ref[0]
    first, second = tile1_ref[...], tile2_ref[...]
    before, after = jnp.where(even, first, second), jnp.where(even, second, first)
    k_ref[...] = jnp.where(offset == -1, before, jnp.where(offset == 1, after, own_ref[...]))
    fine = d_ref.shape[0]
    step = ynear_ref.shape[0] // fine
    fz = yside_ref.shape[1] // 2
    for n in range(fine):
        rows = slice(n * step, (n + 1) * step)
        halo = jnp.concatenate([ynear_ref[rows], yfar_ref[rows]], axis=0)
        more = jnp.dot(add_ref[parity("gy")], halo, preferred_element_type=F32)
        ends = (at(n, fine, yside_ref, ysidee_ref) + more[: 2 * fz]).astype(BF16)
        side_ref[n] = at(n, fine, zside_ref, zsidee_ref) + more[2 * fz :]
        phi_ref[n] = jnp.concatenate([ends[:fz], at(n, fine, mid_ref, mide_ref), ends[fz:]], axis=0)
    for n in range(fine):
        d_ref[n : n + 1] = row_of(slot_sums(phi_ref[n], k_ref[...], 128))


def finish_kernel(near_ref, far_ref, side_ref, d_ref, tile_ref, out_ref):
    fine, cells = d_ref.shape
    even = parity("gz") == 0
    fy = near_ref.shape[0] // fine
    fz = cells // fy
    shape = (2 * fy, cells)
    row, lane = lax.broadcasted_iota(jnp.int32, shape, 0), lax.broadcasted_iota(jnp.int32, shape, 1)
    mine = lane == jnp.where(row < fy, row * fz, (row - fy) * fz + fz - 1)
    lane = lax.broadcasted_iota(jnp.int32, (1, cells), 1) % fz
    side = (lane == 0) | (lane == fz - 1)
    some = fine // 4
    for part in range(4):
        phi = []
        for n in range(part * some, (part + 1) * some):
            near, far = near_ref[n * fy : (n + 1) * fy].astype(F32), far_ref[n * fy : (n + 1) * fy].astype(F32)
            before, after = jnp.where(even, far, near), jnp.where(even, near, far)
            phi.append((side_ref[n] + jnp.concatenate([before, after], axis=0)).astype(BF16))
        sums = slot_sums(jnp.concatenate(phi, axis=0), tile_ref[...], cells)
        for i in range(some):
            n = part * some + i
            new = jnp.sum(jnp.where(mine, sums[i * 2 * fy : (i + 1) * 2 * fy], 0.0), axis=0, keepdims=True)
            new = jnp.where(side, new, d_ref[n : n + 1])
            for j in range(cells // 128):
                out_ref[n * (cells // 128) + j : n * (cells // 128) + j + 1] = new[:, j * 128 : (j + 1) * 128]


def call(body, outs, args, scalars=0, scratch=(), flops=1e6, hbm=()):
    space = lambda i: pltpu.SMEM if i < scalars else pltpu.HBM if i in hbm else pltpu.VMEM
    specs = [pl.BlockSpec(memory_space=space(i)) for i in range(len(args))]
    args = [a if i < scalars else pltpu.with_memory_space_constraint(a, space(i)) for i, a in enumerate(args)]
    size = sum(int(np.prod(o.shape)) * o.dtype.itemsize for o in outs)
    return pl.pallas_call(
        body,
        out_shape=tuple(outs),
        in_specs=specs,
        out_specs=tuple(pl.BlockSpec(memory_space=pltpu.VMEM) for _ in outs),
        scratch_shapes=list(scratch),
        compiler_params=pltpu.CompilerParams(vmem_limit_bytes=16 << 20),
        cost_estimate=pl.CostEstimate(flops=int(flops), bytes_accessed=size, transcendentals=0),
    )(*args)


def send(value, pairs):
    return lax.ppermute(value, AXES, pairs)


def body(coefficients, fun_count, tile_offset, kernel, *, shape):
    return steps(coefficients, fun_count, tile_offset, kernel, shape)


def steps(coefficients, fun_count, tile_offset, kernel, shape):
    bands, cx, cy, cz, slots = coefficients.shape
    text, mzh, add = make_tables(cy, cz)
    rows, cells, fx = cy * cz, 4 * cy * cz, 2 * cx
    near = [swap_pairs(shape, axis, True) for axis in range(3)]
    far = [swap_pairs(shape, axis, False) for axis in range(3)]
    vmem = pltpu.VMEM
    count = fun_count.reshape(1)
    offset = tile_offset.reshape(1)
    c = coefficients.reshape(bands, cx, rows, slots)
    own = kernel.reshape(kernel.shape[1:])
    face = vmem((4 * rows, slots), BF16)

    xnear, xfar, planes, text = call(
        faces_kernel, [face, face, vmem((2, bands, rows, slots), BF16), vmem(text.shape[1:], BF16)], [count, c, text], 1,
        scratch=[pltpu.SemaphoreType.DMA((3,))], hbm=(1, 2),
    )
    xfar = send(xfar, far[0])
    xnear = send(xnear, near[0])
    up_pairs, down1_pairs, down2_pairs = round_pairs(shape)
    up = send(own, up_pairs)
    down = send(own, down1_pairs)

    def cell_outs(n):
        return [
            vmem((n, cells - 4 * cz, slots), BF16), vmem((n, 4 * cz, slots), F32),
            vmem((n, 4 * cy, slots), F32), vmem((n, 4 * cy, slots), F32),
        ]

    x, mid, yside, z, zside = call(
        inner_kernel, [vmem((fx - 2, 4 * rows, slots), BF16)] + cell_outs(fx - 2), [count, c, text], 1,
        flops=2e9,
    )
    yshape = vmem((fx * 2 * cz, slots), BF16)
    edge, ynear, yfar = call(
        functools.partial(edge_kernel, cy=cy, cz=cz),
        [vmem((2, 4 * rows, slots), BF16), yshape, yshape], [count, planes, xnear, xfar, x], 1,
    )
    yfar = send(yfar, far[1])
    ynear = send(ynear, near[1])
    down = send(down, down2_pairs)
    tile1 = send(own, tile_pairs(shape))
    mide, ysidee, ze, zsidee = call(edge_cells_kernel, cell_outs(2), [edge, text], flops=3e8)
    zshape = vmem((fx * 2 * cy, slots), BF16)
    znear, zfar = call(zfaces_kernel, [zshape, zshape], [ynear, yfar, z, ze, mzh])
    znear = send(znear, near[2])
    zfar = send(zfar, far[2])
    tile1 = tile1 + up + down
    tile2 = send(tile1, near[1])
    side, d, tile = call(
        density_kernel, [vmem((fx, 4 * cy, slots), F32), vmem((fx, cells), F32), vmem((slots, slots), BF16)],
        [offset, own, tile1, tile2, ynear, yfar, add, mid, yside, zside, mide, ysidee, zsidee], 1, flops=2e9,
        scratch=[vmem((fx, cells, slots), BF16)],
    )
    (out,) = call(finish_kernel, [jax.ShapeDtypeStruct((fx * cells // 128, 128), F32)], [znear, zfar, side, d, tile])
    return out.reshape(1, 1, 1, -1)


def solution(mesh):
    placed = (
        P(None, "gx", "gy", "gz", None),
        P("gx", "gy", "gz"),
        P("gx", "gy", "gz"),
        P("gx", None, None),
    )
    shape = tuple(mesh.shape[a] for a in AXES)
    return jax.shard_map(
        functools.partial(body, shape=shape), mesh=mesh, in_specs=placed, out_specs=P("gx", "gy", "gz", None), check_vma=False
    )
```

```python
import functools

import jax
import jax.numpy as jnp
import ml_dtypes
import numpy as np
from jax import lax
from jax.experimental import pallas as pl
from jax.experimental.pallas import tpu as pltpu
from jax.sharding import PartitionSpec as P


FILT = [0.48296291314453416, 0.8365163037378079, 0.2241438680420134, -0.12940952255126037]
WAVE = [(1.0 if t % 2 == 0 else -1.0) * FILT[3 - t] for t in range(4)]
AXES = ("gx", "gy", "gz")
F32, BF16 = jnp.float32, jnp.bfloat16


def band_table(coarse):
    table = np.zeros((2, 2 * coarse, coarse))
    for fine in range(2 * coarse):
        for point in range(coarse):
            tap = fine - 2 * point + 1
            if 0 <= tap <= 3:
                table[0, fine, point] = FILT[tap]
                table[1, fine, point] = WAVE[tap]
    return table


def make_tables(cy, cz):
    ty, tz = band_table(cy), band_table(cz)
    fy, fz = 2 * cy, 2 * cz
    inner = np.einsum("cnk,dml->nmcdkl", ty, tz).reshape(fy, fz, 4 * cy * cz)
    zside = np.concatenate([inner[:, 0], inner[:, fz - 1]])
    inner = inner.reshape(fy * fz, 4 * cy * cz)
    ends = {}
    for name, plane, tap in (("first", 0, 0), ("last", cz - 1, 3)):
        pick = np.zeros((2, cz))
        pick[0, plane], pick[1, plane] = FILT[tap], WAVE[tap]
        own = np.einsum("cnk,dl->ncdkl", ty, pick).reshape(fy, 4 * cy * cz)
        before = np.zeros((fy, 2 * cz))
        before[0] = pick.reshape(-1)
        after = np.zeros((fy, 2 * cz))
        after[fy - 1] = pick.reshape(-1)
        ends[name] = (own, before, after)
    along = np.transpose(tz, (1, 0, 2)).reshape(fz, 2 * cz)
    adds = {}
    for name, row in (("before", 0), ("after", fy - 1)):
        rows = np.zeros((2, fz, 2 * cz))
        rows[0 if name == "before" else 1] = along
        sides = np.zeros((2, fy, 2 * cz))
        sides[0, row], sides[1, row] = along[0], along[fz - 1]
        adds[name] = np.concatenate([rows.reshape(2 * fz, -1), sides.reshape(2 * fy, -1)])
    text, mzh, add = [], [], []
    which = {"before": 1, "after": 2}
    for pz in range(2):
        order = ("last", "first") if pz == 0 else ("first", "last")
        text.append(np.concatenate([inner] + [ends[o][0] for o in order] + [zside]))
    for py in range(2):
        sides = ("after", "before") if py == 0 else ("before", "after")
        add.append(np.concatenate([adds[s] for s in sides], axis=1))
        for pz in range(2):
            order = ("last", "first") if pz == 0 else ("first", "last")
            mzh.append(np.concatenate([np.concatenate([ends[o][which[s]] for s in sides], axis=1) for o in order]))
    cast = lambda parts: np.stack(parts).astype(np.float32).astype(ml_dtypes.bfloat16)
    return cast(text), cast(mzh), cast(add)


def swap_pairs(shape, axis, near):
    out = []
    for place in np.ndindex(*shape):
        other = list(place)
        other[axis] = place[axis] ^ 1 if near else ((place[axis] - 1) ^ 1) + 1
        if 0 <= other[axis] < shape[axis]:
            out.append((int(np.ravel_multi_index(place, shape)), int(np.ravel_multi_index(other, shape))))
    return out


def tile_pairs(shape):
    nx, ny, _ = shape
    out = []
    for x, y, z in np.ndindex(*shape):
        source = x - 1 if y % 2 == 0 else x + 1
        if 0 <= source < nx:
            place = (source, (y + ny // 2) % ny if source // 4 != x // 4 else y, z)
            out.append((at_place(shape, *place), at_place(shape, x, y, z)))
    return out


def at_place(shape, x, y, z):
    return int(np.ravel_multi_index((x, y, z), shape))


def round_pairs(shape):
    nx, ny, nz = shape
    up, down1, down2 = [], [], []
    stops = ((3, 11, 1, 1), (2, 8, 3, 3))
    for z in range(nz):
        for y in (0, 2):
            up.append((at_place(shape, nx - 1, (y + 2) % ny, z), at_place(shape, 0, y, z)))
        for y, stop_x, stop_y, last_y in stops:
            down1.append((at_place(shape, 0, y, z), at_place(shape, stop_x, stop_y, z)))
            down2.append((at_place(shape, stop_x, stop_y, z), at_place(shape, nx - 1, last_y, z)))
    return up, down1, down2


def parity(axis):
    return lax.rem(lax.axis_index(axis), 2)


def lane_mask(count_ref, rows, lanes):
    return lax.broadcasted_iota(jnp.int32, (rows, lanes), 1) < count_ref[0]


def faces_kernel(count_ref, c_hbm, text_hbm, near_ref, far_ref, planes_ref, text_ref, sem):
    last_k, rows = c_hbm.shape[1] - 1, c_hbm.shape[2]
    copies = [pltpu.make_async_copy(c_hbm.at[:, k], planes_ref.at[i], sem.at[i]) for i, k in enumerate((0, last_k))]
    table = pltpu.make_async_copy(text_hbm.at[parity("gz")], text_ref, sem.at[2])
    for copy in copies:
        copy.start()
    table.start()
    even = parity("gx") == 0
    mask = lane_mask(count_ref, rows, c_hbm.shape[3])
    for copy in copies:
        copy.wait()
    for b in range(4):
        first = FILT[0] * planes_ref[0, b].astype(F32) + WAVE[0] * planes_ref[0, 4 + b].astype(F32)
        last = FILT[3] * planes_ref[1, b].astype(F32) + WAVE[3] * planes_ref[1, 4 + b].astype(F32)
        first, last = jnp.where(mask, first, 0.0), jnp.where(mask, last, 0.0)
        near_ref[b * rows : (b + 1) * rows] = jnp.where(even, last, first).astype(BF16)
        far_ref[b * rows : (b + 1) * rows] = jnp.where(even, first, last).astype(BF16)
    table.wait()


def split_cells(r, i, mid_ref, yside_ref, z_ref, zside_ref):
    fz, sent = yside_ref.shape[1] // 2, z_ref.shape[1]
    cells = mid_ref.shape[1] + 2 * fz
    mid_ref[i] = r[fz : cells - fz].astype(BF16)
    yside_ref[i] = jnp.concatenate([r[:fz], r[cells - fz : cells]], axis=0)
    z_ref[i] = r[cells : cells + sent]
    zside_ref[i] = r[cells + sent :]


def inner_kernel(count_ref, c_ref, text_ref, mid_ref, yside_ref, z_ref, zside_ref):
    planes, rows = c_ref.shape[1], c_ref.shape[2]
    mask = lane_mask(count_ref, rows, c_ref.shape[3])
    for m in range(1, planes):
        odd, even = [], []
        for b in range(4):
            s0, w0 = c_ref[b, m - 1].astype(F32), c_ref[4 + b, m - 1].astype(F32)
            s1, w1 = c_ref[b, m].astype(F32), c_ref[4 + b, m].astype(F32)
            o = FILT[2] * s0 + WAVE[2] * w0 + FILT[0] * s1 + WAVE[0] * w1
            e = FILT[3] * s0 + WAVE[3] * w0 + FILT[1] * s1 + WAVE[1] * w1
            odd.append(jnp.where(mask, o, 0.0).astype(BF16))
            even.append(jnp.where(mask, e, 0.0).astype(BF16))
        for i, parts in ((2 * m - 2, odd), (2 * m - 1, even)):
            x = jnp.concatenate(parts, axis=0)
            split_cells(jnp.dot(text_ref[...], x, preferred_element_type=F32), i, mid_ref, yside_ref, z_ref, zside_ref)


def rim_kernel(count_ref, c_ref, ynear_ref, yfar_ref, *, cz):
    planes, rows = c_ref.shape[1], c_ref.shape[2]
    mask = lane_mask(count_ref, cz, c_ref.shape[3])
    even_y = parity("gy") == 0
    ends = []
    for tap, low in ((3, rows - cz), (0, 0)):
        end = [[None] * planes for _ in range(4)]
        for xb in range(2):
            for zb in range(2):
                for k in range(planes):
                    s0 = c_ref[4 * xb + zb, k, low : low + cz].astype(F32)
                    w0 = c_ref[4 * xb + 2 + zb, k, low : low + cz].astype(F32)
                    end[2 * xb + zb][k] = jnp.where(mask, FILT[tap] * s0 + WAVE[tap] * w0, 0.0)
        ends.append(end)
    for m in range(1, planes):
        for n, old, new in ((2 * m - 1, 2, 0), (2 * m, 3, 1)):
            sides = []
            for end in ends:
                parts = []
                for zb in range(2):
                    s, w = end[zb], end[2 + zb]
                    parts.append(FILT[old] * s[m - 1] + WAVE[old] * w[m - 1] + FILT[new] * s[m] + WAVE[new] * w[m])
                sides.append(jnp.concatenate(parts, axis=0))
            last, first = sides
            ynear_ref[n * 2 * cz : (n + 1) * 2 * cz] = jnp.where(even_y, last, first).astype(BF16)
            yfar_ref[n * 2 * cz : (n + 1) * 2 * cz] = jnp.where(even_y, first, last).astype(BF16)


def edge_kernel(count_ref, planes_ref, near_ref, far_ref, nearrim_ref, farrim_ref, edge_ref, ynear_ref, yfar_ref, *, cy, cz):
    rows = planes_ref.shape[2]
    mask = lane_mask(count_ref, rows, planes_ref.shape[3])
    even = parity("gx") == 0
    for b in range(4):
        near, far = near_ref[b * rows : (b + 1) * rows].astype(F32), far_ref[b * rows : (b + 1) * rows].astype(F32)
        before, after = jnp.where(even, far, near), jnp.where(even, near, far)
        s0, w0 = planes_ref[0, b].astype(F32), planes_ref[0, 4 + b].astype(F32)
        s1, w1 = planes_ref[1, b].astype(F32), planes_ref[1, 4 + b].astype(F32)
        lo = jnp.where(mask, FILT[1] * s0 + WAVE[1] * w0, 0.0) + before
        hi = jnp.where(mask, FILT[2] * s1 + WAVE[2] * w1, 0.0) + after
        edge_ref[0, b * rows : (b + 1) * rows] = lo.astype(BF16)
        edge_ref[1, b * rows : (b + 1) * rows] = hi.astype(BF16)
    even_y = parity("gy") == 0
    step, size = 2 * cz, ynear_ref.shape[0]
    ynear_ref[step : size - step] = nearrim_ref[step : size - step]
    yfar_ref[step : size - step] = farrim_ref[step : size - step]
    for i, start in ((0, 0), (1, size - step)):
        near_rows, far_rows = [], []
        for zb in range(2):
            low, high = zb * rows, (2 + zb) * rows
            end = (cy - 1) * cz
            face = lambda tap, at: FILT[tap] * edge_ref[i, low + at : low + at + cz].astype(F32) + WAVE[tap] * edge_ref[i, high + at : high + at + cz].astype(F32)
            first, last = face(0, 0), face(3, end)
            near_rows.append(jnp.where(even_y, last, first))
            far_rows.append(jnp.where(even_y, first, last))
        ynear_ref[start : start + step] = jnp.concatenate(near_rows, axis=0).astype(BF16)
        yfar_ref[start : start + step] = jnp.concatenate(far_rows, axis=0).astype(BF16)


def edge_cells_kernel(edge_ref, text_ref, *out_refs):
    for i in range(2):
        split_cells(jnp.dot(text_ref[...], edge_ref[i], preferred_element_type=F32), i, *out_refs)


def at(n, fine, inner_ref, edge_ref):
    return edge_ref[0] if n == 0 else edge_ref[1] if n == fine - 1 else inner_ref[n - 1]


def zfaces_kernel(ynear_ref, yfar_ref, z_ref, ze_ref, mzh_ref, near_ref, far_ref):
    case = 2 * parity("gy") + parity("gz")
    fine = z_ref.shape[0] + 2
    step = ynear_ref.shape[0] // fine
    half = z_ref.shape[1] // 2
    for n in range(fine):
        rows = slice(n * step, (n + 1) * step)
        halo = jnp.concatenate([ynear_ref[rows], yfar_ref[rows]], axis=0)
        r = at(n, fine, z_ref, ze_ref) + jnp.dot(mzh_ref[case], halo, preferred_element_type=F32)
        near_ref[n * half : (n + 1) * half] = r[:half].astype(BF16)
        far_ref[n * half : (n + 1) * half] = r[half:].astype(BF16)


def slot_sums(phi, k, wide):
    psi = jnp.dot(phi, k, preferred_element_type=F32)
    prod = phi.astype(F32) * psi
    half = prod.shape[1] // 2
    prod = prod[:, :half] + prod[:, half:]
    high = prod.astype(BF16)
    low = (prod - high.astype(F32)).astype(BF16)
    return jnp.dot(jnp.concatenate([high, low], axis=1), jnp.ones((2 * half, wide), BF16), preferred_element_type=F32)


def row_of(sums):
    lanes = sums.shape[1]
    diag = lax.broadcasted_iota(jnp.int32, (lanes, lanes), 0) == lax.broadcasted_iota(jnp.int32, (lanes, lanes), 1)
    parts = [jnp.where(diag, sums[i : i + lanes], 0.0) for i in range(0, sums.shape[0], lanes)]
    return jnp.concatenate([jnp.sum(part, axis=0, keepdims=True) for part in parts], axis=1)


def density_kernel(offset_ref, own_ref, tile1_ref, tile2_ref, ynear_ref, yfar_ref, add_ref, *rest):
    mid_ref, yside_ref, zside_ref, mide_ref, ysidee_ref, zsidee_ref, side_ref, d_ref, k_ref, phi_ref = rest
    even = parity("gy") == 0
    offset = offset_ref[0]
    first, second = tile1_ref[...], tile2_ref[...]
    before, after = jnp.where(even, first, second), jnp.where(even, second, first)
    k_ref[...] = jnp.where(offset == -1, before, jnp.where(offset == 1, after, own_ref[...]))
    fine = d_ref.shape[0]
    step = ynear_ref.shape[0] // fine
    fz = yside_ref.shape[1] // 2
    for n in range(fine):
        rows = slice(n * step, (n + 1) * step)
        halo = jnp.concatenate([ynear_ref[rows], yfar_ref[rows]], axis=0)
        more = jnp.dot(add_ref[parity("gy")], halo, preferred_element_type=F32)
        ends = (at(n, fine, yside_ref, ysidee_ref) + more[: 2 * fz]).astype(BF16)
        side_ref[n] = at(n, fine, zside_ref, zsidee_ref) + more[2 * fz :]
        phi_ref[n] = jnp.concatenate([ends[:fz], at(n, fine, mid_ref, mide_ref), ends[fz:]], axis=0)
    for n in range(fine):
        d_ref[n : n + 1] = row_of(slot_sums(phi_ref[n], k_ref[...], 128))


def finish_kernel(near_ref, far_ref, side_ref, d_ref, tile_ref, out_ref):
    fine, cells = d_ref.shape
    even = parity("gz") == 0
    fy = near_ref.shape[0] // fine
    fz = cells // fy
    shape = (2 * fy, cells)
    row, lane = lax.broadcasted_iota(jnp.int32, shape, 0), lax.broadcasted_iota(jnp.int32, shape, 1)
    mine = lane == jnp.where(row < fy, row * fz, (row - fy) * fz + fz - 1)
    lane = lax.broadcasted_iota(jnp.int32, (1, cells), 1) % fz
    side = (lane == 0) | (lane == fz - 1)
    some = fine // 4
    for part in range(4):
        phi = []
        for n in range(part * some, (part + 1) * some):
            near, far = near_ref[n * fy : (n + 1) * fy].astype(F32), far_ref[n * fy : (n + 1) * fy].astype(F32)
            before, after = jnp.where(even, far, near), jnp.where(even, near, far)
            phi.append((side_ref[n] + jnp.concatenate([before, after], axis=0)).astype(BF16))
        sums = slot_sums(jnp.concatenate(phi, axis=0), tile_ref[...], cells)
        for i in range(some):
            n = part * some + i
            new = jnp.sum(jnp.where(mine, sums[i * 2 * fy : (i + 1) * 2 * fy], 0.0), axis=0, keepdims=True)
            new = jnp.where(side, new, d_ref[n : n + 1])
            for j in range(cells // 128):
                out_ref[n * (cells // 128) + j : n * (cells // 128) + j + 1] = new[:, j * 128 : (j + 1) * 128]


def call(body, outs, args, scalars=0, scratch=(), flops=1e6, hbm=()):
    space = lambda i: pltpu.SMEM if i < scalars else pltpu.HBM if i in hbm else pltpu.VMEM
    specs = [pl.BlockSpec(memory_space=space(i)) for i in range(len(args))]
    args = [a if i < scalars else pltpu.with_memory_space_constraint(a, space(i)) for i, a in enumerate(args)]
    size = sum(int(np.prod(o.shape)) * o.dtype.itemsize for o in outs)
    return pl.pallas_call(
        body,
        out_shape=tuple(outs),
        in_specs=specs,
        out_specs=tuple(pl.BlockSpec(memory_space=pltpu.VMEM) for _ in outs),
        scratch_shapes=list(scratch),
        compiler_params=pltpu.CompilerParams(vmem_limit_bytes=16 << 20),
        cost_estimate=pl.CostEstimate(flops=int(flops), bytes_accessed=size, transcendentals=0),
    )(*args)


def send(value, pairs):
    return lax.ppermute(value, AXES, pairs)


def body(coefficients, fun_count, tile_offset, kernel, *, shape):
    return steps(coefficients, fun_count, tile_offset, kernel, shape)


def steps(coefficients, fun_count, tile_offset, kernel, shape):
    bands, cx, cy, cz, slots = coefficients.shape
    text, mzh, add = make_tables(cy, cz)
    rows, cells, fx = cy * cz, 4 * cy * cz, 2 * cx
    near = [swap_pairs(shape, axis, True) for axis in range(3)]
    far = [swap_pairs(shape, axis, False) for axis in range(3)]
    vmem = pltpu.VMEM
    count = fun_count.reshape(1)
    offset = tile_offset.reshape(1)
    c = coefficients.reshape(bands, cx, rows, slots)
    own = kernel.reshape(kernel.shape[1:])
    face = vmem((4 * rows, slots), BF16)

    xnear, xfar, planes, text = call(
        faces_kernel, [face, face, vmem((2, bands, rows, slots), BF16), vmem(text.shape[1:], BF16)], [count, c, text], 1,
        scratch=[pltpu.SemaphoreType.DMA((3,))], hbm=(1, 2),
    )
    xfar = send(xfar, far[0])
    xnear = send(xnear, near[0])
    up_pairs, down1_pairs, down2_pairs = round_pairs(shape)
    up = send(own, up_pairs)
    down = send(own, down1_pairs)

    def cell_outs(n):
        return [
            vmem((n, cells - 4 * cz, slots), BF16), vmem((n, 4 * cz, slots), F32),
            vmem((n, 4 * cy, slots), F32), vmem((n, 4 * cy, slots), F32),
        ]

    yshape = vmem((fx * 2 * cz, slots), BF16)
    nearrim, farrim = call(functools.partial(rim_kernel, cz=cz), [yshape, yshape], [count, c], 1)
    mid, yside, z, zside = call(inner_kernel, cell_outs(fx - 2), [count, c, text], 1, flops=2e9)
    edge, ynear, yfar = call(
        functools.partial(edge_kernel, cy=cy, cz=cz),
        [vmem((2, 4 * rows, slots), BF16), yshape, yshape], [count, planes, xnear, xfar, nearrim, farrim], 1,
    )
    yfar = send(yfar, far[1])
    ynear = send(ynear, near[1])
    down = send(down, down2_pairs)
    tile1 = send(own, tile_pairs(shape))
    mide, ysidee, ze, zsidee = call(edge_cells_kernel, cell_outs(2), [edge, text], flops=3e8)
    zshape = vmem((fx * 2 * cy, slots), BF16)
    znear, zfar = call(zfaces_kernel, [zshape, zshape], [ynear, yfar, z, ze, mzh])
    znear = send(znear, near[2])
    zfar = send(zfar, far[2])
    tile1 = tile1 + up + down
    tile2 = send(tile1, near[1])
    side, d, tile = call(
        density_kernel, [vmem((fx, 4 * cy, slots), F32), vmem((fx, cells), F32), vmem((slots, slots), BF16)],
        [offset, own, tile1, tile2, ynear, yfar, add, mid, yside, zside, mide, ysidee, zsidee], 1, flops=2e9,
        scratch=[vmem((fx, cells, slots), BF16)],
    )
    (out,) = call(finish_kernel, [jax.ShapeDtypeStruct((fx * cells // 128, 128), F32)], [znear, zfar, side, d, tile])
    return out.reshape(1, 1, 1, -1)


def solution(mesh):
    placed = (
        P(None, "gx", "gy", "gz", None),
        P("gx", "gy", "gz"),
        P("gx", "gy", "gz"),
        P("gx", None, None),
    )
    shape = tuple(mesh.shape[a] for a in AXES)
    return jax.shard_map(
        functools.partial(body, shape=shape), mesh=mesh, in_specs=placed, out_specs=P("gx", "gy", "gz", None), check_vma=False
    )
```

```python
import functools

import jax
import jax.numpy as jnp
import ml_dtypes
import numpy as np
from jax import lax
from jax.experimental import pallas as pl
from jax.experimental.pallas import tpu as pltpu
from jax.sharding import PartitionSpec as P


FILT = [0.48296291314453416, 0.8365163037378079, 0.2241438680420134, -0.12940952255126037]
WAVE = [(1.0 if t % 2 == 0 else -1.0) * FILT[3 - t] for t in range(4)]
AXES = ("gx", "gy", "gz")
F32, BF16 = jnp.float32, jnp.bfloat16


def band_table(coarse):
    table = np.zeros((2, 2 * coarse, coarse))
    for fine in range(2 * coarse):
        for point in range(coarse):
            tap = fine - 2 * point + 1
            if 0 <= tap <= 3:
                table[0, fine, point] = FILT[tap]
                table[1, fine, point] = WAVE[tap]
    return table


def make_tables(cy, cz):
    ty, tz = band_table(cy), band_table(cz)
    fy, fz = 2 * cy, 2 * cz
    inner = np.einsum("cnk,dml->nmcdkl", ty, tz).reshape(fy, fz, 4 * cy * cz)
    zside = np.concatenate([inner[:, 0], inner[:, fz - 1]])
    inner = inner.reshape(fy * fz, 4 * cy * cz)
    ends = {}
    for name, plane, tap in (("first", 0, 0), ("last", cz - 1, 3)):
        pick = np.zeros((2, cz))
        pick[0, plane], pick[1, plane] = FILT[tap], WAVE[tap]
        own = np.einsum("cnk,dl->ncdkl", ty, pick).reshape(fy, 4 * cy * cz)
        before = np.zeros((fy, 2 * cz))
        before[0] = pick.reshape(-1)
        after = np.zeros((fy, 2 * cz))
        after[fy - 1] = pick.reshape(-1)
        ends[name] = (own, before, after)
    along = np.transpose(tz, (1, 0, 2)).reshape(fz, 2 * cz)
    adds = {}
    for name, row in (("before", 0), ("after", fy - 1)):
        rows = np.zeros((2, fz, 2 * cz))
        rows[0 if name == "before" else 1] = along
        sides = np.zeros((2, fy, 2 * cz))
        sides[0, row], sides[1, row] = along[0], along[fz - 1]
        adds[name] = np.concatenate([rows.reshape(2 * fz, -1), sides.reshape(2 * fy, -1)])
    text, mzh, add = [], [], []
    which = {"before": 1, "after": 2}
    for pz in range(2):
        order = ("last", "first") if pz == 0 else ("first", "last")
        text.append(np.concatenate([inner] + [ends[o][0] for o in order] + [zside]))
    for py in range(2):
        sides = ("after", "before") if py == 0 else ("before", "after")
        add.append(np.concatenate([adds[s] for s in sides], axis=1))
        for pz in range(2):
            order = ("last", "first") if pz == 0 else ("first", "last")
            mzh.append(np.concatenate([np.concatenate([ends[o][which[s]] for s in sides], axis=1) for o in order]))
    cast = lambda parts: np.stack(parts).astype(np.float32).astype(ml_dtypes.bfloat16)
    return cast(text), cast(mzh), cast(add)


def swap_pairs(shape, axis, near):
    out = []
    for place in np.ndindex(*shape):
        other = list(place)
        other[axis] = place[axis] ^ 1 if near else ((place[axis] - 1) ^ 1) + 1
        if 0 <= other[axis] < shape[axis]:
            out.append((int(np.ravel_multi_index(place, shape)), int(np.ravel_multi_index(other, shape))))
    return out


def tile_pairs(shape):
    nx, ny, _ = shape
    out = []
    for x, y, z in np.ndindex(*shape):
        source = x - 1 if y % 2 == 0 else x + 1
        if 0 <= source < nx:
            place = (source, (y + ny // 2) % ny if source // 4 != x // 4 else y, z)
            out.append((at_place(shape, *place), at_place(shape, x, y, z)))
    return out


def at_place(shape, x, y, z):
    return int(np.ravel_multi_index((x, y, z), shape))


def round_pairs(shape):
    nx, ny, nz = shape
    up, down1, down2 = [], [], []
    stops = ((3, 11, 1, 1), (2, 8, 3, 3))
    for z in range(nz):
        for y in (0, 2):
            up.append((at_place(shape, nx - 1, (y + 2) % ny, z), at_place(shape, 0, y, z)))
        for y, stop_x, stop_y, last_y in stops:
            down1.append((at_place(shape, 0, y, z), at_place(shape, stop_x, stop_y, z)))
            down2.append((at_place(shape, stop_x, stop_y, z), at_place(shape, nx - 1, last_y, z)))
    return up, down1, down2


def parity(axis):
    return lax.rem(lax.axis_index(axis), 2)


def lane_mask(count_ref, rows, lanes):
    return lax.broadcasted_iota(jnp.int32, (rows, lanes), 1) < count_ref[0]


def faces_kernel(count_ref, c_hbm, text_hbm, near_ref, far_ref, planes_ref, text_ref, sem):
    last_k, rows = c_hbm.shape[1] - 1, c_hbm.shape[2]
    copies = [pltpu.make_async_copy(c_hbm.at[:, k], planes_ref.at[i], sem.at[i]) for i, k in enumerate((0, last_k))]
    table = pltpu.make_async_copy(text_hbm.at[parity("gz")], text_ref, sem.at[2])
    for copy in copies:
        copy.start()
    table.start()
    even = parity("gx") == 0
    mask = lane_mask(count_ref, rows, c_hbm.shape[3])
    for copy in copies:
        copy.wait()
    for b in range(4):
        first = FILT[0] * planes_ref[0, b].astype(F32) + WAVE[0] * planes_ref[0, 4 + b].astype(F32)
        last = FILT[3] * planes_ref[1, b].astype(F32) + WAVE[3] * planes_ref[1, 4 + b].astype(F32)
        first, last = jnp.where(mask, first, 0.0), jnp.where(mask, last, 0.0)
        near_ref[b * rows : (b + 1) * rows] = jnp.where(even, last, first).astype(BF16)
        far_ref[b * rows : (b + 1) * rows] = jnp.where(even, first, last).astype(BF16)
    table.wait()


def split_cells(r, i, mid_ref, yside_ref, z_ref, zside_ref):
    fz, sent = yside_ref.shape[1] // 2, z_ref.shape[1]
    cells = mid_ref.shape[1] + 2 * fz
    mid_ref[i] = r[fz : cells - fz].astype(BF16)
    yside_ref[i] = jnp.concatenate([r[:fz], r[cells - fz : cells]], axis=0)
    z_ref[i] = r[cells : cells + sent]
    zside_ref[i] = r[cells + sent :]


def inner_kernel(count_ref, c_ref, text_ref, mid_ref, yside_ref, z_ref, zside_ref):
    planes, rows = c_ref.shape[1], c_ref.shape[2]
    mask = lane_mask(count_ref, rows, c_ref.shape[3])
    for m in range(1, planes):
        odd, even = [], []
        for b in range(4):
            s0, w0 = c_ref[b, m - 1].astype(F32), c_ref[4 + b, m - 1].astype(F32)
            s1, w1 = c_ref[b, m].astype(F32), c_ref[4 + b, m].astype(F32)
            o = FILT[2] * s0 + WAVE[2] * w0 + FILT[0] * s1 + WAVE[0] * w1
            e = FILT[3] * s0 + WAVE[3] * w0 + FILT[1] * s1 + WAVE[1] * w1
            odd.append(jnp.where(mask, o, 0.0).astype(BF16))
            even.append(jnp.where(mask, e, 0.0).astype(BF16))
        for i, parts in ((2 * m - 2, odd), (2 * m - 1, even)):
            x = jnp.concatenate(parts, axis=0)
            split_cells(jnp.dot(text_ref[...], x, preferred_element_type=F32), i, mid_ref, yside_ref, z_ref, zside_ref)


def rim_kernel(count_ref, c_ref, ynear_ref, yfar_ref, *, cz):
    planes, rows = c_ref.shape[1], c_ref.shape[2]
    mask = lane_mask(count_ref, cz, c_ref.shape[3])
    even_y = parity("gy") == 0
    ends = []
    for tap, low in ((3, rows - cz), (0, 0)):
        end = [[None] * planes for _ in range(4)]
        for xb in range(2):
            for zb in range(2):
                for k in range(planes):
                    s0 = c_ref[4 * xb + zb, k, low : low + cz].astype(F32)
                    w0 = c_ref[4 * xb + 2 + zb, k, low : low + cz].astype(F32)
                    end[2 * xb + zb][k] = jnp.where(mask, FILT[tap] * s0 + WAVE[tap] * w0, 0.0)
        ends.append(end)
    for m in range(1, planes):
        for n, old, new in ((2 * m - 1, 2, 0), (2 * m, 3, 1)):
            sides = []
            for end in ends:
                parts = []
                for zb in range(2):
                    s, w = end[zb], end[2 + zb]
                    parts.append(FILT[old] * s[m - 1] + WAVE[old] * w[m - 1] + FILT[new] * s[m] + WAVE[new] * w[m])
                sides.append(jnp.concatenate(parts, axis=0))
            last, first = sides
            ynear_ref[n * 2 * cz : (n + 1) * 2 * cz] = jnp.where(even_y, last, first).astype(BF16)
            yfar_ref[n * 2 * cz : (n + 1) * 2 * cz] = jnp.where(even_y, first, last).astype(BF16)


def edge_kernel(count_ref, planes_ref, near_ref, far_ref, nearrim_ref, farrim_ref, edge_ref, ynear_ref, yfar_ref, *, cy, cz):
    rows = planes_ref.shape[2]
    mask = lane_mask(count_ref, rows, planes_ref.shape[3])
    even = parity("gx") == 0
    for b in range(4):
        near, far = near_ref[b * rows : (b + 1) * rows].astype(F32), far_ref[b * rows : (b + 1) * rows].astype(F32)
        before, after = jnp.where(even, far, near), jnp.where(even, near, far)
        s0, w0 = planes_ref[0, b].astype(F32), planes_ref[0, 4 + b].astype(F32)
        s1, w1 = planes_ref[1, b].astype(F32), planes_ref[1, 4 + b].astype(F32)
        lo = jnp.where(mask, FILT[1] * s0 + WAVE[1] * w0, 0.0) + before
        hi = jnp.where(mask, FILT[2] * s1 + WAVE[2] * w1, 0.0) + after
        edge_ref[0, b * rows : (b + 1) * rows] = lo.astype(BF16)
        edge_ref[1, b * rows : (b + 1) * rows] = hi.astype(BF16)
    even_y = parity("gy") == 0
    step, size = 2 * cz, ynear_ref.shape[0]
    ynear_ref[step : size - step] = nearrim_ref[step : size - step]
    yfar_ref[step : size - step] = farrim_ref[step : size - step]
    for i, start in ((0, 0), (1, size - step)):
        near_rows, far_rows = [], []
        for zb in range(2):
            low, high = zb * rows, (2 + zb) * rows
            end = (cy - 1) * cz
            face = lambda tap, at: FILT[tap] * edge_ref[i, low + at : low + at + cz].astype(F32) + WAVE[tap] * edge_ref[i, high + at : high + at + cz].astype(F32)
            first, last = face(0, 0), face(3, end)
            near_rows.append(jnp.where(even_y, last, first))
            far_rows.append(jnp.where(even_y, first, last))
        ynear_ref[start : start + step] = jnp.concatenate(near_rows, axis=0).astype(BF16)
        yfar_ref[start : start + step] = jnp.concatenate(far_rows, axis=0).astype(BF16)


def edge_cells_kernel(edge_ref, text_ref, *out_refs):
    for i in range(2):
        split_cells(jnp.dot(text_ref[...], edge_ref[i], preferred_element_type=F32), i, *out_refs)


def at(n, fine, inner_ref, edge_ref):
    return edge_ref[0] if n == 0 else edge_ref[1] if n == fine - 1 else inner_ref[n - 1]


def zfaces_kernel(ynear_ref, yfar_ref, z_ref, ze_ref, mzh_ref, near_ref, far_ref):
    case = 2 * parity("gy") + parity("gz")
    fine = z_ref.shape[0] + 2
    step = ynear_ref.shape[0] // fine
    half = z_ref.shape[1] // 2
    for n in range(fine):
        rows = slice(n * step, (n + 1) * step)
        halo = jnp.concatenate([ynear_ref[rows], yfar_ref[rows]], axis=0)
        r = at(n, fine, z_ref, ze_ref) + jnp.dot(mzh_ref[case], halo, preferred_element_type=F32)
        near_ref[n * half : (n + 1) * half] = r[:half].astype(BF16)
        far_ref[n * half : (n + 1) * half] = r[half:].astype(BF16)


def slot_sums(phi, k, wide):
    psi = jnp.dot(phi, k, preferred_element_type=F32)
    prod = phi.astype(F32) * psi
    half = prod.shape[1] // 2
    prod = prod[:, :half] + prod[:, half:]
    high = prod.astype(BF16)
    low = (prod - high.astype(F32)).astype(BF16)
    return jnp.dot(jnp.concatenate([high, low], axis=1), jnp.ones((2 * half, wide), BF16), preferred_element_type=F32)


def row_of(sums):
    lanes = sums.shape[1]
    diag = lax.broadcasted_iota(jnp.int32, (lanes, lanes), 0) == lax.broadcasted_iota(jnp.int32, (lanes, lanes), 1)
    parts = [jnp.where(diag, sums[i : i + lanes], 0.0) for i in range(0, sums.shape[0], lanes)]
    return jnp.concatenate([jnp.sum(part, axis=0, keepdims=True) for part in parts], axis=1)


def density_kernel(offset_ref, own_ref, tile1_ref, tile2_ref, ynear_ref, yfar_ref, add_ref, *rest):
    mid_ref, yside_ref, zside_ref, mide_ref, ysidee_ref, zsidee_ref, side_ref, d_ref, k_ref, phi_ref = rest
    even = parity("gy") == 0
    offset = offset_ref[0]
    first, second = tile1_ref[...], tile2_ref[...]
    before, after = jnp.where(even, first, second), jnp.where(even, second, first)
    k_ref[...] = jnp.where(offset == -1, before, jnp.where(offset == 1, after, own_ref[...]))
    fine = d_ref.shape[0]
    step = ynear_ref.shape[0] // fine
    fz = yside_ref.shape[1] // 2
    for n in range(fine):
        rows = slice(n * step, (n + 1) * step)
        halo = jnp.concatenate([ynear_ref[rows], yfar_ref[rows]], axis=0)
        more = jnp.dot(add_ref[parity("gy")], halo, preferred_element_type=F32)
        ends = (at(n, fine, yside_ref, ysidee_ref) + more[: 2 * fz]).astype(BF16)
        side_ref[n] = at(n, fine, zside_ref, zsidee_ref) + more[2 * fz :]
        phi_ref[n] = jnp.concatenate([ends[:fz], at(n, fine, mid_ref, mide_ref), ends[fz:]], axis=0)
    for n in range(fine):
        d_ref[n : n + 1] = row_of(slot_sums(phi_ref[n], k_ref[...], 128))


def finish_kernel(near_ref, far_ref, side_ref, d_ref, tile_ref, out_ref):
    fine, cells = d_ref.shape
    even = parity("gz") == 0
    fy = near_ref.shape[0] // fine
    fz = cells // fy
    shape = (2 * fy, cells)
    row, lane = lax.broadcasted_iota(jnp.int32, shape, 0), lax.broadcasted_iota(jnp.int32, shape, 1)
    mine = lane == jnp.where(row < fy, row * fz, (row - fy) * fz + fz - 1)
    lane = lax.broadcasted_iota(jnp.int32, (1, cells), 1) % fz
    side = (lane == 0) | (lane == fz - 1)
    some = fine // 4
    for part in range(4):
        phi = []
        for n in range(part * some, (part + 1) * some):
            near, far = near_ref[n * fy : (n + 1) * fy].astype(F32), far_ref[n * fy : (n + 1) * fy].astype(F32)
            before, after = jnp.where(even, far, near), jnp.where(even, near, far)
            phi.append((side_ref[n] + jnp.concatenate([before, after], axis=0)).astype(BF16))
        sums = slot_sums(jnp.concatenate(phi, axis=0), tile_ref[...], cells)
        for i in range(some):
            n = part * some + i
            new = jnp.sum(jnp.where(mine, sums[i * 2 * fy : (i + 1) * 2 * fy], 0.0), axis=0, keepdims=True)
            new = jnp.where(side, new, d_ref[n : n + 1])
            for j in range(cells // 128):
                out_ref[n * (cells // 128) + j : n * (cells // 128) + j + 1] = new[:, j * 128 : (j + 1) * 128]


def call(body, outs, args, scalars=0, scratch=(), flops=1e6, hbm=()):
    space = lambda i: pltpu.SMEM if i < scalars else pltpu.HBM if i in hbm else pltpu.VMEM
    specs = [pl.BlockSpec(memory_space=space(i)) for i in range(len(args))]
    args = [a if i < scalars else pltpu.with_memory_space_constraint(a, space(i)) for i, a in enumerate(args)]
    size = sum(int(np.prod(o.shape)) * o.dtype.itemsize for o in outs)
    return pl.pallas_call(
        body,
        out_shape=tuple(outs),
        in_specs=specs,
        out_specs=tuple(pl.BlockSpec(memory_space=pltpu.VMEM) for _ in outs),
        scratch_shapes=list(scratch),
        compiler_params=pltpu.CompilerParams(vmem_limit_bytes=16 << 20),
        cost_estimate=pl.CostEstimate(flops=int(flops), bytes_accessed=size, transcendentals=0),
    )(*args)


def send(value, pairs):
    return lax.ppermute(value, AXES, pairs)


def body(coefficients, fun_count, tile_offset, kernel, *, shape):
    return steps(coefficients, fun_count, tile_offset, kernel, shape)


def steps(coefficients, fun_count, tile_offset, kernel, shape):
    bands, cx, cy, cz, slots = coefficients.shape
    text, mzh, add = make_tables(cy, cz)
    rows, cells, fx = cy * cz, 4 * cy * cz, 2 * cx
    near = [swap_pairs(shape, axis, True) for axis in range(3)]
    far = [swap_pairs(shape, axis, False) for axis in range(3)]
    vmem = pltpu.VMEM
    count = fun_count.reshape(1)
    offset = tile_offset.reshape(1)
    c = coefficients.reshape(bands, cx, rows, slots)
    own = kernel.reshape(kernel.shape[1:])
    face = vmem((4 * rows, slots), BF16)

    xnear, xfar, planes, text = call(
        faces_kernel, [face, face, vmem((2, bands, rows, slots), BF16), vmem(text.shape[1:], BF16)], [count, c, text], 1,
        scratch=[pltpu.SemaphoreType.DMA((3,))], hbm=(1, 2),
    )
    xfar = send(xfar, far[0])
    xnear = send(xnear, near[0])
    up_pairs, down1_pairs, down2_pairs = round_pairs(shape)
    down = send(own, down1_pairs)

    def cell_outs(n):
        return [
            vmem((n, cells - 4 * cz, slots), BF16), vmem((n, 4 * cz, slots), F32),
            vmem((n, 4 * cy, slots), F32), vmem((n, 4 * cy, slots), F32),
        ]

    yshape = vmem((fx * 2 * cz, slots), BF16)
    nearrim, farrim = call(functools.partial(rim_kernel, cz=cz), [yshape, yshape], [count, c], 1)
    mid, yside, z, zside = call(inner_kernel, cell_outs(fx - 2), [count, c, text], 1, flops=2e9)
    edge, ynear, yfar = call(
        functools.partial(edge_kernel, cy=cy, cz=cz),
        [vmem((2, 4 * rows, slots), BF16), yshape, yshape], [count, planes, xnear, xfar, nearrim, farrim], 1,
    )
    yfar = send(yfar, far[1])
    ynear = send(ynear, near[1])
    down = send(down, down2_pairs)
    tile1 = send(own, tile_pairs(shape) + up_pairs)
    mide, ysidee, ze, zsidee = call(edge_cells_kernel, cell_outs(2), [edge, text], flops=3e8)
    zshape = vmem((fx * 2 * cy, slots), BF16)
    znear, zfar = call(zfaces_kernel, [zshape, zshape], [ynear, yfar, z, ze, mzh])
    znear = send(znear, near[2])
    zfar = send(zfar, far[2])
    tile1 = tile1 + down
    tile2 = send(tile1, near[1])
    side, d, tile = call(
        density_kernel, [vmem((fx, 4 * cy, slots), F32), vmem((fx, cells), F32), vmem((slots, slots), BF16)],
        [offset, own, tile1, tile2, ynear, yfar, add, mid, yside, zside, mide, ysidee, zsidee], 1, flops=2e9,
        scratch=[vmem((fx, cells, slots), BF16)],
    )
    (out,) = call(finish_kernel, [jax.ShapeDtypeStruct((fx * cells // 128, 128), F32)], [znear, zfar, side, d, tile])
    return out.reshape(1, 1, 1, -1)


def solution(mesh):
    placed = (
        P(None, "gx", "gy", "gz", None),
        P("gx", "gy", "gz"),
        P("gx", "gy", "gz"),
        P("gx", None, None),
    )
    shape = tuple(mesh.shape[a] for a in AXES)
    return jax.shard_map(
        functools.partial(body, shape=shape), mesh=mesh, in_specs=placed, out_specs=P("gx", "gy", "gz", None), check_vma=False
    )
```

```python
import functools

import jax
import jax.numpy as jnp
import ml_dtypes
import numpy as np
from jax import lax
from jax.experimental import pallas as pl
from jax.experimental.pallas import tpu as pltpu
from jax.sharding import PartitionSpec as P


FILT = [0.48296291314453416, 0.8365163037378079, 0.2241438680420134, -0.12940952255126037]
WAVE = [(1.0 if t % 2 == 0 else -1.0) * FILT[3 - t] for t in range(4)]
AXES = ("gx", "gy", "gz")
F32, BF16 = jnp.float32, jnp.bfloat16


def band_table(coarse):
    table = np.zeros((2, 2 * coarse, coarse))
    for fine in range(2 * coarse):
        for point in range(coarse):
            tap = fine - 2 * point + 1
            if 0 <= tap <= 3:
                table[0, fine, point] = FILT[tap]
                table[1, fine, point] = WAVE[tap]
    return table


def make_tables(cy, cz):
    ty, tz = band_table(cy), band_table(cz)
    fy, fz = 2 * cy, 2 * cz
    inner = np.einsum("cnk,dml->nmcdkl", ty, tz).reshape(fy, fz, 4 * cy * cz)
    zside = np.concatenate([inner[:, 0], inner[:, fz - 1]])
    inner = inner.reshape(fy * fz, 4 * cy * cz)
    ends = {}
    for name, plane, tap in (("first", 0, 0), ("last", cz - 1, 3)):
        pick = np.zeros((2, cz))
        pick[0, plane], pick[1, plane] = FILT[tap], WAVE[tap]
        own = np.einsum("cnk,dl->ncdkl", ty, pick).reshape(fy, 4 * cy * cz)
        before = np.zeros((fy, 2 * cz))
        before[0] = pick.reshape(-1)
        after = np.zeros((fy, 2 * cz))
        after[fy - 1] = pick.reshape(-1)
        ends[name] = (own, before, after)
    along = np.transpose(tz, (1, 0, 2)).reshape(fz, 2 * cz)
    adds = {}
    for name, row in (("before", 0), ("after", fy - 1)):
        rows = np.zeros((2, fz, 2 * cz))
        rows[0 if name == "before" else 1] = along
        sides = np.zeros((2, fy, 2 * cz))
        sides[0, row], sides[1, row] = along[0], along[fz - 1]
        adds[name] = np.concatenate([rows.reshape(2 * fz, -1), sides.reshape(2 * fy, -1)])
    text, mzh, add = [], [], []
    which = {"before": 1, "after": 2}
    for pz in range(2):
        order = ("last", "first") if pz == 0 else ("first", "last")
        text.append(np.concatenate([inner] + [ends[o][0] for o in order] + [zside]))
    for py in range(2):
        sides = ("after", "before") if py == 0 else ("before", "after")
        add.append(np.concatenate([adds[s] for s in sides], axis=1))
        for pz in range(2):
            order = ("last", "first") if pz == 0 else ("first", "last")
            mzh.append(np.concatenate([np.concatenate([ends[o][which[s]] for s in sides], axis=1) for o in order]))
    cast = lambda parts: np.stack(parts).astype(np.float32).astype(ml_dtypes.bfloat16)
    return cast(text), cast(mzh), cast(add)


def swap_pairs(shape, axis, near):
    out = []
    for place in np.ndindex(*shape):
        other = list(place)
        other[axis] = place[axis] ^ 1 if near else ((place[axis] - 1) ^ 1) + 1
        if 0 <= other[axis] < shape[axis]:
            out.append((int(np.ravel_multi_index(place, shape)), int(np.ravel_multi_index(other, shape))))
    return out


def tile_pairs(shape):
    nx, ny, _ = shape
    out = []
    for x, y, z in np.ndindex(*shape):
        source = x - 1 if y % 2 == 0 else x + 1
        if 0 <= source < nx:
            place = (source, (y + ny // 2) % ny if source // 4 != x // 4 else y, z)
            out.append((at_place(shape, *place), at_place(shape, x, y, z)))
    return out


def at_place(shape, x, y, z):
    return int(np.ravel_multi_index((x, y, z), shape))


def round_pairs(shape):
    nx, ny, nz = shape
    up, down1, down2 = [], [], []
    stops = ((3, 11, 1, 1), (2, 8, 3, 3))
    for z in range(nz):
        for y in (0, 2):
            up.append((at_place(shape, nx - 1, (y + 2) % ny, z), at_place(shape, 0, y, z)))
        for y, stop_x, stop_y, last_y in stops:
            down1.append((at_place(shape, 0, y, z), at_place(shape, stop_x, stop_y, z)))
            down2.append((at_place(shape, stop_x, stop_y, z), at_place(shape, nx - 1, last_y, z)))
    return up, down1, down2


def parity(axis):
    return lax.rem(lax.axis_index(axis), 2)


def lane_mask(count_ref, rows, lanes):
    return lax.broadcasted_iota(jnp.int32, (rows, lanes), 1) < count_ref[0]


def faces_kernel(count_ref, c_hbm, text_hbm, near_ref, far_ref, planes_ref, text_ref, sem):
    last_k, rows = c_hbm.shape[1] - 1, c_hbm.shape[2]
    copies = [pltpu.make_async_copy(c_hbm.at[:, k], planes_ref.at[i], sem.at[i]) for i, k in enumerate((0, last_k))]
    table = pltpu.make_async_copy(text_hbm.at[parity("gz")], text_ref, sem.at[2])
    for copy in copies:
        copy.start()
    table.start()
    even = parity("gx") == 0
    mask = lane_mask(count_ref, rows, c_hbm.shape[3])
    for copy in copies:
        copy.wait()
    for b in range(4):
        first = FILT[0] * planes_ref[0, b].astype(F32) + WAVE[0] * planes_ref[0, 4 + b].astype(F32)
        last = FILT[3] * planes_ref[1, b].astype(F32) + WAVE[3] * planes_ref[1, 4 + b].astype(F32)
        first, last = jnp.where(mask, first, 0.0), jnp.where(mask, last, 0.0)
        near_ref[b * rows : (b + 1) * rows] = jnp.where(even, last, first).astype(BF16)
        far_ref[b * rows : (b + 1) * rows] = jnp.where(even, first, last).astype(BF16)
    table.wait()


def split_cells(r, i, mid_ref, yside_ref, z_ref, zside_ref):
    fz, sent = yside_ref.shape[1] // 2, z_ref.shape[1]
    cells = mid_ref.shape[1] + 2 * fz
    mid_ref[i] = r[fz : cells - fz].astype(BF16)
    yside_ref[i] = jnp.concatenate([r[:fz], r[cells - fz : cells]], axis=0)
    z_ref[i] = r[cells : cells + sent]
    zside_ref[i] = r[cells + sent :]


def inner_kernel(count_ref, c_ref, text_ref, mid_ref, yside_ref, z_ref, zside_ref):
    planes, rows = c_ref.shape[1], c_ref.shape[2]
    mask = lane_mask(count_ref, rows, c_ref.shape[3])
    for m in range(1, planes):
        odd, even = [], []
        for b in range(4):
            s0, w0 = c_ref[b, m - 1].astype(F32), c_ref[4 + b, m - 1].astype(F32)
            s1, w1 = c_ref[b, m].astype(F32), c_ref[4 + b, m].astype(F32)
            o = FILT[2] * s0 + WAVE[2] * w0 + FILT[0] * s1 + WAVE[0] * w1
            e = FILT[3] * s0 + WAVE[3] * w0 + FILT[1] * s1 + WAVE[1] * w1
            odd.append(jnp.where(mask, o, 0.0).astype(BF16))
            even.append(jnp.where(mask, e, 0.0).astype(BF16))
        for i, parts in ((2 * m - 2, odd), (2 * m - 1, even)):
            x = jnp.concatenate(parts, axis=0)
            split_cells(jnp.dot(text_ref[...], x, preferred_element_type=F32), i, mid_ref, yside_ref, z_ref, zside_ref)


def rim_kernel(count_ref, c_ref, ynear_ref, yfar_ref, *, cz):
    planes, rows = c_ref.shape[1], c_ref.shape[2]
    mask = lane_mask(count_ref, cz, c_ref.shape[3])
    even_y = parity("gy") == 0
    ends = []
    for tap, low in ((3, rows - cz), (0, 0)):
        end = [[None] * planes for _ in range(4)]
        for xb in range(2):
            for zb in range(2):
                for k in range(planes):
                    s0 = c_ref[4 * xb + zb, k, low : low + cz].astype(F32)
                    w0 = c_ref[4 * xb + 2 + zb, k, low : low + cz].astype(F32)
                    end[2 * xb + zb][k] = jnp.where(mask, FILT[tap] * s0 + WAVE[tap] * w0, 0.0)
        ends.append(end)
    for m in range(1, planes):
        for n, old, new in ((2 * m - 1, 2, 0), (2 * m, 3, 1)):
            sides = []
            for end in ends:
                parts = []
                for zb in range(2):
                    s, w = end[zb], end[2 + zb]
                    parts.append(FILT[old] * s[m - 1] + WAVE[old] * w[m - 1] + FILT[new] * s[m] + WAVE[new] * w[m])
                sides.append(jnp.concatenate(parts, axis=0))
            last, first = sides
            ynear_ref[n * 2 * cz : (n + 1) * 2 * cz] = jnp.where(even_y, last, first).astype(BF16)
            yfar_ref[n * 2 * cz : (n + 1) * 2 * cz] = jnp.where(even_y, first, last).astype(BF16)


def edge_kernel(count_ref, planes_ref, near_ref, far_ref, nearrim_ref, farrim_ref, edge_ref, ynear_ref, yfar_ref, *, cy, cz):
    rows = planes_ref.shape[2]
    mask = lane_mask(count_ref, rows, planes_ref.shape[3])
    even = parity("gx") == 0
    for b in range(4):
        near, far = near_ref[b * rows : (b + 1) * rows].astype(F32), far_ref[b * rows : (b + 1) * rows].astype(F32)
        before, after = jnp.where(even, far, near), jnp.where(even, near, far)
        s0, w0 = planes_ref[0, b].astype(F32), planes_ref[0, 4 + b].astype(F32)
        s1, w1 = planes_ref[1, b].astype(F32), planes_ref[1, 4 + b].astype(F32)
        lo = jnp.where(mask, FILT[1] * s0 + WAVE[1] * w0, 0.0) + before
        hi = jnp.where(mask, FILT[2] * s1 + WAVE[2] * w1, 0.0) + after
        edge_ref[0, b * rows : (b + 1) * rows] = lo.astype(BF16)
        edge_ref[1, b * rows : (b + 1) * rows] = hi.astype(BF16)
    even_y = parity("gy") == 0
    step, size = 2 * cz, ynear_ref.shape[0]
    ynear_ref[step : size - step] = nearrim_ref[step : size - step]
    yfar_ref[step : size - step] = farrim_ref[step : size - step]
    for i, start in ((0, 0), (1, size - step)):
        near_rows, far_rows = [], []
        for zb in range(2):
            low, high = zb * rows, (2 + zb) * rows
            end = (cy - 1) * cz
            face = lambda tap, at: FILT[tap] * edge_ref[i, low + at : low + at + cz].astype(F32) + WAVE[tap] * edge_ref[i, high + at : high + at + cz].astype(F32)
            first, last = face(0, 0), face(3, end)
            near_rows.append(jnp.where(even_y, last, first))
            far_rows.append(jnp.where(even_y, first, last))
        ynear_ref[start : start + step] = jnp.concatenate(near_rows, axis=0).astype(BF16)
        yfar_ref[start : start + step] = jnp.concatenate(far_rows, axis=0).astype(BF16)


def edge_cells_kernel(edge_ref, text_ref, *out_refs):
    for i in range(2):
        split_cells(jnp.dot(text_ref[...], edge_ref[i], preferred_element_type=F32), i, *out_refs)


def at(n, fine, inner_ref, edge_ref):
    return edge_ref[0] if n == 0 else edge_ref[1] if n == fine - 1 else inner_ref[n - 1]


def zfaces_kernel(ynear_ref, yfar_ref, z_ref, ze_ref, mzh_ref, near_ref, far_ref):
    case = 2 * parity("gy") + parity("gz")
    fine = z_ref.shape[0] + 2
    step = ynear_ref.shape[0] // fine
    half = z_ref.shape[1] // 2
    for n in range(fine):
        rows = slice(n * step, (n + 1) * step)
        halo = jnp.concatenate([ynear_ref[rows], yfar_ref[rows]], axis=0)
        r = at(n, fine, z_ref, ze_ref) + jnp.dot(mzh_ref[case], halo, preferred_element_type=F32)
        near_ref[n * half : (n + 1) * half] = r[:half].astype(BF16)
        far_ref[n * half : (n + 1) * half] = r[half:].astype(BF16)


def slot_sums(phi, k, wide):
    psi = jnp.dot(phi, k, preferred_element_type=F32)
    prod = phi.astype(F32) * psi
    half = prod.shape[1] // 2
    prod = prod[:, :half] + prod[:, half:]
    high = prod.astype(BF16)
    low = (prod - high.astype(F32)).astype(BF16)
    return jnp.dot(jnp.concatenate([high, low], axis=1), jnp.ones((2 * half, wide), BF16), preferred_element_type=F32)


def row_of(sums):
    lanes = sums.shape[1]
    diag = lax.broadcasted_iota(jnp.int32, (lanes, lanes), 0) == lax.broadcasted_iota(jnp.int32, (lanes, lanes), 1)
    parts = [jnp.where(diag, sums[i : i + lanes], 0.0) for i in range(0, sums.shape[0], lanes)]
    return jnp.concatenate([jnp.sum(part, axis=0, keepdims=True) for part in parts], axis=1)


def density_kernel(offset_ref, own_ref, tile1_ref, tile2_ref, ynear_ref, yfar_ref, add_ref, *rest):
    mid_ref, yside_ref, zside_ref, mide_ref, ysidee_ref, zsidee_ref, side_ref, d_ref, k_ref, phi_ref = rest
    even = parity("gy") == 0
    offset = offset_ref[0]
    first, second = tile1_ref[...], tile2_ref[...]
    before, after = jnp.where(even, first, second), jnp.where(even, second, first)
    k_ref[...] = jnp.where(offset == -1, before, jnp.where(offset == 1, after, own_ref[...]))
    fine = d_ref.shape[0]
    step = ynear_ref.shape[0] // fine
    fz = yside_ref.shape[1] // 2
    for n in range(fine):
        rows = slice(n * step, (n + 1) * step)
        halo = jnp.concatenate([ynear_ref[rows], yfar_ref[rows]], axis=0)
        more = jnp.dot(add_ref[parity("gy")], halo, preferred_element_type=F32)
        ends = (at(n, fine, yside_ref, ysidee_ref) + more[: 2 * fz]).astype(BF16)
        side_ref[n] = at(n, fine, zside_ref, zsidee_ref) + more[2 * fz :]
        phi_ref[n] = jnp.concatenate([ends[:fz], at(n, fine, mid_ref, mide_ref), ends[fz:]], axis=0)
    for n in range(fine):
        d_ref[n : n + 1] = row_of(slot_sums(phi_ref[n], k_ref[...], 128))


def side_kernel(got_ref, side_ref, d_ref, tile_ref, out_ref, *, near):
    fine, cells = d_ref.shape
    last = parity("gz") == (0 if near else 1)
    fy = got_ref.shape[0] // fine
    fz = cells // fy
    edge = jnp.where(last, fz - 1, 0)
    row, lane = (lax.broadcasted_iota(jnp.int32, (fy, cells), axis) for axis in range(2))
    mine = lane == row * fz + edge
    at_edge = lax.broadcasted_iota(jnp.int32, (1, cells), 1) % fz == edge
    some = fine // 2
    for part in range(2):
        phi = []
        for n in range(part * some, (part + 1) * some):
            own = jnp.where(last, side_ref[n, fy:], side_ref[n, :fy])
            phi.append((own + got_ref[n * fy : (n + 1) * fy].astype(F32)).astype(BF16))
        sums = slot_sums(jnp.concatenate(phi, axis=0), tile_ref[...], cells)
        for i in range(some):
            n = part * some + i
            new = jnp.sum(jnp.where(mine, sums[i * fy : (i + 1) * fy], 0.0), axis=0, keepdims=True)
            new = jnp.where(at_edge, new, d_ref[n : n + 1])
            width = out_ref.shape[1]
            for j in range(cells // width):
                out_ref[n * (cells // width) + j : n * (cells // width) + j + 1] = new[:, j * width : (j + 1) * width]


def call(body, outs, args, scalars=0, scratch=(), flops=1e6, hbm=()):
    space = lambda i: pltpu.SMEM if i < scalars else pltpu.HBM if i in hbm else pltpu.VMEM
    specs = [pl.BlockSpec(memory_space=space(i)) for i in range(len(args))]
    args = [a if i < scalars else pltpu.with_memory_space_constraint(a, space(i)) for i, a in enumerate(args)]
    size = sum(int(np.prod(o.shape)) * o.dtype.itemsize for o in outs)
    return pl.pallas_call(
        body,
        out_shape=tuple(outs),
        in_specs=specs,
        out_specs=tuple(pl.BlockSpec(memory_space=pltpu.VMEM) for _ in outs),
        scratch_shapes=list(scratch),
        compiler_params=pltpu.CompilerParams(vmem_limit_bytes=16 << 20),
        cost_estimate=pl.CostEstimate(flops=int(flops), bytes_accessed=size, transcendentals=0),
    )(*args)


def send(value, pairs):
    return lax.ppermute(value, AXES, pairs)


def body(coefficients, fun_count, tile_offset, kernel, *, shape):
    return steps(coefficients, fun_count, tile_offset, kernel, shape)


def steps(coefficients, fun_count, tile_offset, kernel, shape):
    bands, cx, cy, cz, slots = coefficients.shape
    text, mzh, add = make_tables(cy, cz)
    rows, cells, fx = cy * cz, 4 * cy * cz, 2 * cx
    near = [swap_pairs(shape, axis, True) for axis in range(3)]
    far = [swap_pairs(shape, axis, False) for axis in range(3)]
    vmem = pltpu.VMEM
    count = fun_count.reshape(1)
    offset = tile_offset.reshape(1)
    c = coefficients.reshape(bands, cx, rows, slots)
    own = kernel.reshape(kernel.shape[1:])
    face = vmem((4 * rows, slots), BF16)

    xnear, xfar, planes, text = call(
        faces_kernel, [face, face, vmem((2, bands, rows, slots), BF16), vmem(text.shape[1:], BF16)], [count, c, text], 1,
        scratch=[pltpu.SemaphoreType.DMA((3,))], hbm=(1, 2),
    )
    xfar = send(xfar, far[0])
    xnear = send(xnear, near[0])
    up_pairs, down1_pairs, down2_pairs = round_pairs(shape)
    down = send(own, down1_pairs)

    def cell_outs(n):
        return [
            vmem((n, cells - 4 * cz, slots), BF16), vmem((n, 4 * cz, slots), F32),
            vmem((n, 4 * cy, slots), F32), vmem((n, 4 * cy, slots), F32),
        ]

    yshape = vmem((fx * 2 * cz, slots), BF16)
    nearrim, farrim = call(functools.partial(rim_kernel, cz=cz), [yshape, yshape], [count, c], 1)
    mid, yside, z, zside = call(inner_kernel, cell_outs(fx - 2), [count, c, text], 1, flops=2e9)
    edge, ynear, yfar = call(
        functools.partial(edge_kernel, cy=cy, cz=cz),
        [vmem((2, 4 * rows, slots), BF16), yshape, yshape], [count, planes, xnear, xfar, nearrim, farrim], 1,
    )
    yfar = send(yfar, far[1])
    ynear = send(ynear, near[1])
    down = send(down, down2_pairs)
    tile1 = send(own, tile_pairs(shape) + up_pairs)
    mide, ysidee, ze, zsidee = call(edge_cells_kernel, cell_outs(2), [edge, text], flops=3e8)
    zshape = vmem((fx * 2 * cy, slots), BF16)
    znear, zfar = call(zfaces_kernel, [zshape, zshape], [ynear, yfar, z, ze, mzh])
    znear = send(znear, near[2])
    zfar = send(zfar, far[2])
    tile1 = tile1 + down
    tile2 = send(tile1, near[1])
    side, d, tile = call(
        density_kernel, [vmem((fx, 4 * cy, slots), F32), vmem((fx, cells), F32), vmem((slots, slots), BF16)],
        [offset, own, tile1, tile2, ynear, yfar, add, mid, yside, zside, mide, ysidee, zsidee], 1, flops=2e9,
        scratch=[vmem((fx, cells, slots), BF16)],
    )
    (d,) = call(functools.partial(side_kernel, near=True), [vmem((fx, cells), F32)], [znear, side, d, tile])
    (out,) = call(
        functools.partial(side_kernel, near=False), [jax.ShapeDtypeStruct((fx * cells // 128, 128), F32)], [zfar, side, d, tile]
    )
    return out.reshape(1, 1, 1, -1)


def solution(mesh):
    placed = (
        P(None, "gx", "gy", "gz", None),
        P("gx", "gy", "gz"),
        P("gx", "gy", "gz"),
        P("gx", None, None),
    )
    shape = tuple(mesh.shape[a] for a in AXES)
    return jax.shard_map(
        functools.partial(body, shape=shape), mesh=mesh, in_specs=placed, out_specs=P("gx", "gy", "gz", None), check_vma=False
    )
```
